32 devices in a mesh: row: 8 (over y, x, core), col: 4 (over z).
Axes of the slice: x: 2, y: 2, z: 4, core: 2. Of those that a mesh axis runs over, the one named last changes fastest.
Arguments:
- ingest: bfloat16 [2048, 8192], P(('row', 'col')), may hold values from -128 to 127, as said below
- row_order: int32 [8, 256], P('row'), may hold values from 0 to 255, each once within a row
- matrix_seeds: int32 [2], replicated, may hold values from 0 to 46336
Outputs:
- second_hint: float32 [4, 2, 1024, 1024], P(None, None, 'col')
The draws below stay inside these ranges and needn't reach their ends.
Inputs may be any that keep to these rules, and one draw needn't show every extreme that they name: `ingest`: integers. `row_order`: each row is a permutation of 0 to 255.
All inputs are finite; a program needn't handle non-finite values.
Results may differ from the reference program's by a relative error of at most 0.0003.
Values may be sent and summed in bfloat16 or wider, within the bound.
No kernel may reach another device: no remote copies, remote signals or barrier semaphores. Data moves between devices by JAX's collectives and lax.ppermute only.
A program may use at most 64 MiB of HBM per device.

```python
import jax
import jax.numpy as jnp
from jax import lax

N = 1024
RD = 256
ROWS = 2048
COLS = 8192
RBLK = 8


def draw_ingest(key, part):
    values = jax.random.randint(key, (ROWS, COLS), -128, 128, dtype=jnp.int32)
    return values.astype(jnp.float32).astype(jnp.bfloat16)


def setup_inputs(seed: int = 0) -> dict:
    seeds = jax.random.split(jax.random.key(seed), 4)
    ingest = draw_ingest(jax.random.fold_in(seeds[3], 71), 0)
    row_order = jax.vmap(lambda own: jax.random.permutation(own, RD))(jax.random.split(seeds[1], RBLK)).reshape((RBLK, RD)).astype(jnp.int32)
    matrix_seeds = jax.random.randint(seeds[2], (2,), 0, 46337).astype(jnp.int32)
    return dict(ingest=ingest, row_order=row_order, matrix_seeds=matrix_seeds)


prime_base = 46337
half_scale = 65536.0


def mixed_value(first_index, second_index, seed_value):
    mixed = (first_index % prime_base * 40503 % prime_base + seed_value) % prime_base
    mixed = (mixed * mixed % prime_base + second_index % prime_base * 29989 % prime_base) % prime_base
    return (mixed * mixed % prime_base + 12345) % prime_base


def seeded_quad(first_index, second_index, seed_value):
    first_mix = mixed_value(first_index, second_index, seed_value)
    second_mix = mixed_value(first_index, second_index, seed_value + 7919)
    pieces = [first_mix % 256, first_mix // 256, second_mix % 256, second_mix // 256]
    return [(piece - 128).astype(jnp.float32).astype(jnp.bfloat16) for piece in pieces]


def combine_limbs(products):
    total = products[0].astype(jnp.int32)
    for place in range(1, 4):
        total = total + products[place].astype(jnp.int32) * jnp.int32(256 ** place)
    return total


def signed_bytes(value):
    return [((lax.shift_right_logical(value, jnp.int32(8 * place)) & 255) - 128).astype(jnp.float32).astype(jnp.bfloat16) for place in range(4)]


def halves(value):
    low_half = (value & 65535).astype(jnp.float32)
    high_half = lax.shift_right_logical(value, jnp.int32(16)).astype(jnp.float32)
    return low_half, high_half


def reference(ingest, row_order, matrix_seeds):
    row_total, col_total = ingest.shape
    col_index = lax.broadcasted_iota(jnp.int32, (col_total, N), 0)
    n_index = lax.broadcasted_iota(jnp.int32, (col_total, N), 1)
    quad_one = jnp.stack(seeded_quad(col_index, n_index, matrix_seeds[0]))
    col_width = min(512, col_total)

    def block_hint(block_number):
        block_rows = lax.dynamic_slice_in_dim(ingest, block_number * RD, RD, 0)
        block_rows = jnp.take(block_rows, row_order[block_number], axis=0)

        def advance(turn_index, running):
            start_col = (turn_index * col_width).astype(jnp.int32)
            piece = lax.dynamic_slice_in_dim(block_rows, start_col, col_width, 1)
            quad_slice = lax.dynamic_slice_in_dim(quad_one, start_col, col_width, 1)
            products = [jnp.dot(piece, quad_slice[place], preferred_element_type=jnp.float32) for place in range(4)]
            return running + combine_limbs(products)

        return lax.fori_loop(0, col_total // col_width, advance, jnp.zeros((RD, N), jnp.int32))

    hint = lax.map(block_hint, jnp.arange(row_total // RD, dtype=jnp.int32)).reshape(row_total, N)
    digits = jnp.stack(signed_bytes(hint))
    row_index = lax.broadcasted_iota(jnp.int32, (row_total, N), 0)
    m_index = lax.broadcasted_iota(jnp.int32, (row_total, N), 1)
    quad_two = jnp.stack(seeded_quad(row_index, m_index, matrix_seeds[1]))
    row_width = min(512, row_total)

    def accumulate(turn_index, running):
        start_row = (turn_index * row_width).astype(jnp.int32)
        quad_slice = lax.dynamic_slice_in_dim(quad_two, start_row, row_width, 1)
        digit_block = lax.dynamic_slice_in_dim(digits, start_row, row_width, 1)
        terms = []
        for digit_place in range(4):
            products = [jnp.dot(quad_slice[place].T, digit_block[digit_place], preferred_element_type=jnp.float32) for place in range(4)]
            terms.append(combine_limbs(products))
        return running + jnp.stack(terms, axis=1)

    total = lax.fori_loop(0, row_total // row_width, accumulate, jnp.zeros((N, 4, N), jnp.int32))
    total = jnp.transpose(total, (1, 2, 0))
    low_half, high_half = halves(total)
    return jnp.stack([low_half, high_half], axis=1) / half_scale
```

```python
import functools

import jax
import jax.numpy as jnp
import numpy as np
from jax import lax
from jax.experimental import pallas as pl
from jax.experimental.pallas import tpu as pltpu
from jax.sharding import PartitionSpec as P

N = 1024

PRIME = 46337
HALF_PRIME = PRIME // 2
WHOLE = (1 << 32) // PRIME
PART = (1 << 32) / PRIME - WHOLE
SCALE = np.float32(PRIME / 2.0**32)
FINE = np.float32(1.5 * 2.0**23)
OFFSET = 32896 - HALF_PRIME
COARSE = np.float32(1.5 * 2.0**31 - 1.5 * 2.0**23 - OFFSET)
FINE_OFFSET = np.float32(1.5 * 2.0**23 + OFFSET)
SUBLANES = 16
LANES = 128
NT = (((1,), (1,)), ((), ()))


def centred(value):
    return value - jnp.where(value > HALF_PRIME, PRIME, 0)


def fixed(value):
    value = centred(value)
    return value * WHOLE + jnp.round(value.astype(jnp.float32) * np.float32(PART)).astype(jnp.int32)


def first_vectors(index, seed, step):
    factor = 2 * (29989 * step % PRIME) % PRIME
    vectors = []
    for extra in (0, 7919):
        inner = (index % PRIME * 40503 % PRIME + (seed + extra)) % PRIME
        a = inner * inner % PRIME
        vectors += [
            centred(a),
            fixed((a * a % PRIME + (12345 - HALF_PRIME + PRIME)) % PRIME),
            fixed(a * factor % PRIME),
        ]
    return vectors


def second_vectors(index, step):
    shift = 29989 * step % PRIME
    b = index % PRIME * 29989 % PRIME
    slope = b * (2 * shift % PRIME) % PRIME + shift * shift % PRIME
    return [fixed(2 * b % PRIME), fixed(b * b % PRIME), fixed(slope % PRIME)]


def bend(step):
    value = 2 * (29989 * step % PRIME) ** 2 % PRIME
    value = value - PRIME if value > HALF_PRIME else value
    return np.int32(round(value * 2**32 / PRIME))


def limb_pair(value):
    rounded = value.astype(jnp.float32) * SCALE + FINE
    kept = (rounded + COARSE) - COARSE
    return (rounded - kept).astype(jnp.bfloat16), (kept - FINE_OFFSET).astype(jnp.bfloat16)


def join(products):
    low_p, high_p, low_q, high_q = products
    small = np.float32(1 / 256)
    p = low_p.astype(jnp.int32) + ((high_p * small).astype(jnp.int32) << 8)
    q = low_q.astype(jnp.int32) + ((high_q * small).astype(jnp.int32) << 8)
    return p + (q << 16)


def first_kernel(width, lane, own_ref, peer_ref, first_ref, second_ref, out_ref, even, odd):
    parts, half, _ = out_ref.shape
    total = own_ref.shape[1] // width * parts

    def make(step, limbs):
        chunk, part = step // parts, step % parts
        by_n = [jnp.concatenate([second_ref[i, part]] * (lane // LANES), axis=1) for i in range(3)]
        for t in range(width // lane):
            at = pl.ds(pl.multiple_of(chunk * width + t * lane, lane), lane)
            for mix in range(2):
                a, square, slope = (first_ref[3 * mix + i : 3 * mix + i + 1, at] for i in range(3))
                value = a * by_n[0] + square + by_n[1]
                slope = slope + by_n[2]
                for k in range(half // SUBLANES):
                    low, high = limb_pair(value)
                    top = 2 * mix * half + k * SUBLANES
                    limbs[top : top + SUBLANES, t * lane : (t + 1) * lane] = low
                    limbs[top + half : top + half + SUBLANES, t * lane : (t + 1) * lane] = high
                    value = value + slope
                    slope = slope + bend(SUBLANES)

    def use(step, limbs):
        chunk, part = step // parts, step % parts
        at = pl.ds(pl.multiple_of(chunk * width, width), width)
        records = jnp.concatenate([own_ref[:, at], peer_ref[:, at]], axis=0)
        product = lax.dot_general(limbs[...], records, NT, preferred_element_type=jnp.float32)
        out_ref[part] += join([product[i * half : (i + 1) * half] for i in range(4)])

    out_ref[...] = jnp.zeros_like(out_ref)
    make(0, even)

    @pl.loop(0, total // 2 - 1)
    def _(i):
        use(2 * i, even)
        make(2 * i + 1, odd)
        use(2 * i + 1, odd)
        make(2 * i + 2, even)

    use(total - 2, even)
    make(total - 1, odd)
    use(total - 1, odd)


def first_hint(own, peer, by_first, by_second, parts, half):
    rows, depth = own.shape
    width = min(1024, depth)
    lane = min(512, width)
    return pl.pallas_call(
        functools.partial(first_kernel, width, lane),
        out_shape=jax.ShapeDtypeStruct((parts, half, 2 * rows), jnp.int32),
        in_specs=[pl.BlockSpec(memory_space=pltpu.VMEM)] * 4,
        out_specs=pl.BlockSpec(memory_space=pltpu.VMEM),
        scratch_shapes=[pltpu.VMEM((4 * half, width), jnp.bfloat16)] * 2,
        name="first_hint",
    )(own, peer, by_first, by_second)


def matrix_kernel(columns, group, first_ref, second_ref, *refs):
    out_ref = refs[-1]

    @pl.loop(0, out_ref.shape[1] // group)
    def _(i):
        at = pl.ds(pl.multiple_of(i * group, group), group)
        by_row = first_ref[at, :]
        for mix in range(2):
            a, square, slope = (by_row[:, 3 * mix + i : 3 * mix + i + 1] for i in range(3))
            value = a * second_ref[0:1] + square + second_ref[1:2]
            slope = slope + second_ref[2:3]
            for k in range(columns // LANES):
                low, high = limb_pair(value)
                out_ref[2 * mix, at, k * LANES : (k + 1) * LANES] = low
                out_ref[2 * mix + 1, at, k * LANES : (k + 1) * LANES] = high
                value = value + slope
                slope = slope + bend(LANES)


def second_matrix(by_first, by_second, columns, after=None):
    rows = by_first.shape[0]
    block = min(256, rows)
    return pl.pallas_call(
        functools.partial(matrix_kernel, columns, min(32, block)),
        grid=(rows // block,),
        out_shape=jax.ShapeDtypeStruct((4, rows, columns), jnp.bfloat16),
        in_specs=[
            pl.BlockSpec((block, by_first.shape[1]), lambda i: (i, 0)),
            pl.BlockSpec(by_second.shape, lambda i: (0, 0)),
        ]
        + ([] if after is None else [pl.BlockSpec(memory_space=pl.ANY)]),
        out_specs=pl.BlockSpec((4, block, columns), lambda i: (0, i, 0)),
        name="second_matrix",
    )(by_first, by_second, *([] if after is None else [after]))


def second_kernel(hint_ref, matrix_ref, *refs):
    out_ref, digits = refs[-2:]
    pieces, half, rows = hint_ref.shape

    @pl.when(pl.program_id(0) == 0)
    def _():
        for s in range(pieces):
            hint = hint_ref[s]
            for place in range(4):
                byte = (lax.shift_right_logical(hint, jnp.int32(8 * place)) & 255) - 128
                digits[place * half : (place + 1) * half, s * rows : (s + 1) * rows] = byte.astype(
                    jnp.float32
                ).astype(jnp.bfloat16)

    total = join(
        [
            jnp.dot(digits[...], matrix_ref[i], preferred_element_type=jnp.float32)
            for i in range(4)
        ]
    )
    for place in range(4):
        term = total[place * half : (place + 1) * half]
        out_ref[place] = term if len(refs) == 2 else refs[0][place] + term


def second_hint(hint, matrix, total=None):
    pieces, half, rows = hint.shape
    _, depth, columns = matrix.shape
    block = min(256, columns)
    out_spec = pl.BlockSpec((4, half, block), lambda i: (0, 0, i))
    return pl.pallas_call(
        second_kernel,
        grid=(columns // block,),
        out_shape=jax.ShapeDtypeStruct((4, half, columns), jnp.int32),
        in_specs=[
            pl.BlockSpec(hint.shape, lambda i: (0, 0, 0)),
            pl.BlockSpec((4, depth, block), lambda i: (0, 0, i)),
        ]
        + ([] if total is None else [out_spec]),
        out_specs=out_spec,
        scratch_shapes=[pltpu.VMEM((4 * half, depth), jnp.bfloat16)],
        input_output_aliases={} if total is None else {2: 0},
        cost_estimate=pl.CostEstimate(
            flops=32 * half * depth * columns,
            bytes_accessed=8 * depth * columns + 32 * half * columns,
            transcendentals=0,
        ),
        name="second_hint",
    )(hint, matrix, *([] if total is None else [total]))


def halves_kernel(_, value_ref, *refs):
    out_ref = refs[-1]
    value = value_ref[...]
    scale = np.float32(1 / 65536)
    out_ref[:, 0] = (value & 65535).astype(jnp.float32) * scale
    out_ref[:, 1] = lax.shift_right_logical(value, jnp.int32(16)).astype(jnp.float32) * scale


def write_halves(value, place, out=None):
    digits, half, columns = value.shape
    return pl.pallas_call(
        halves_kernel,
        grid_spec=pltpu.PrefetchScalarGridSpec(
            num_scalar_prefetch=1,
            grid=(digits,),
            in_specs=[pl.BlockSpec((1, half, columns), lambda i, place: (i, 0, 0))]
            + ([] if out is None else [pl.BlockSpec(memory_space=pl.ANY)]),
            out_specs=pl.BlockSpec((1, 2, half, columns), lambda i, place: (i, 0, place[0], 0)),
        ),
        out_shape=jax.ShapeDtypeStruct((digits, 2, 2 * half, columns), jnp.float32),
        input_output_aliases={} if out is None else {2: 0},
        name="write_halves",
    )(place, value, *([] if out is None else [out]))


def shift_by(value, axis, offset):
    return lax.ppermute(value, axis, [(i, i ^ offset) for i in range(lax.axis_size(axis))])


def on_device(ingest, row_order, matrix_seeds):
    row_size, col_size = lax.axis_size("row"), lax.axis_size("col")
    row, col = lax.axis_index("row"), lax.axis_index("col")
    core = row % 2
    rows, depth = ingest.shape
    half = N // col_size // 2

    peer = shift_by(ingest, "row", 1)

    by_first = first_vectors(jnp.arange(depth, dtype=jnp.int32), matrix_seeds[0], SUBLANES)
    by_first = jnp.stack(by_first + by_first[:2])
    first_n = (2 * jnp.arange(col_size, dtype=jnp.int32)[:, None] + core) * half
    n_index = first_n + jnp.arange(SUBLANES, dtype=jnp.int32)[None, :]
    by_second = jnp.stack(second_vectors(n_index, SUBLANES))
    by_second = jnp.broadcast_to(by_second[..., None], by_second.shape + (LANES,))

    hint = first_hint(ingest, peer, by_first, by_second, col_size, half)

    order = row_order[0]
    block_rows = order.shape[0]
    k_index = lax.broadcasted_iota(jnp.int32, (block_rows, block_rows), 1)
    r_index = lax.broadcasted_iota(jnp.int32, (block_rows, block_rows), 0)
    place = jnp.sum(jnp.where(order[None, :] == r_index, k_index, 0), axis=1) + row * block_rows
    place = jnp.concatenate(
        [lax.dynamic_slice_in_dim(place, (col ^ s) * rows, rows) for s in range(col_size)]
    )[None]
    step = 1
    while step < row_size:
        place = jnp.concatenate([place, shift_by(place, "row", step)])
        step *= 2
    place = place.reshape(row_size // 2, 2, col_size, rows).transpose(0, 2, 1, 3)
    by_row = first_vectors(place.reshape(row_size // 2, -1), matrix_seeds[1], LANES)
    by_row = jnp.stack(by_row + by_row[:2], axis=2)
    by_column = second_vectors(jnp.arange(LANES, dtype=jnp.int32), LANES)
    by_column = jnp.stack(by_column + by_column[:1] * 5)

    mine = lax.dynamic_index_in_dim(hint, col, 0, keepdims=False)
    pieces = [mine]
    for s in range(1, col_size):
        piece = lax.dynamic_index_in_dim(hint, col ^ s, 0, keepdims=False)
        pieces.append(shift_by(piece, "col", s))
    pieces = jnp.stack(pieces)
    total = None
    for t in range(row_size // 2):
        matrix = second_matrix(by_row[t], by_column, N, total if t >= 4 else None)
        total = second_hint(shift_by(pieces, "row", 2 * t) if t else pieces, matrix, total)

    other = shift_by(total, "row", 1)
    out = write_halves(total, core[None])
    return write_halves(other, 1 - core[None], out)


def solution(mesh):
    in_specs = (P(("row", "col"), None), P("row", None), P())
    out_specs = P(None, None, "col", None)
    return jax.shard_map(
        on_device, mesh=mesh, in_specs=in_specs, out_specs=out_specs, check_vma=False
    )
```

```python
import functools

import jax
import jax.numpy as jnp
import numpy as np
from jax import lax
from jax.experimental import pallas as pl
from jax.experimental.pallas import tpu as pltpu
from jax.sharding import PartitionSpec as P

N = 1024

PRIME = 46337
HALF_PRIME = PRIME // 2
WHOLE = (1 << 32) // PRIME
PART = (1 << 32) / PRIME - WHOLE
SCALE = np.float32(PRIME / 2.0**32)
FINE = np.float32(1.5 * 2.0**23)
INVERSE = np.float32(1 / PRIME)
OFFSET = 32896 - HALF_PRIME
COARSE = np.float32(1.5 * 2.0**31 - 1.5 * 2.0**23 - OFFSET)
FINE_OFFSET = np.float32(1.5 * 2.0**23 + OFFSET)
SUBLANES = 16
LANES = 128
NT = (((1,), (1,)), ((), ()))


def residue(value):
    value = value - (value.astype(jnp.float32) * INVERSE).astype(jnp.int32) * PRIME
    value = value + jnp.where(value < 0, PRIME, 0)
    return value - jnp.where(value >= PRIME, PRIME, 0)


def centred(value):
    return value - jnp.where(value > HALF_PRIME, PRIME, 0)


def fixed(value):
    value = centred(value)
    return value * WHOLE + jnp.round(value.astype(jnp.float32) * np.float32(PART)).astype(jnp.int32)


def bend(step):
    value = 2 * (29989 * step % PRIME) ** 2 % PRIME
    value = value - PRIME if value > HALF_PRIME else value
    return np.int32(round(value * 2**32 / PRIME))


def by_first(index, seed, step):
    rows = 8
    shape = (rows, index.shape[1])
    row = lax.broadcasted_iota(jnp.int32, shape, 0)
    kind, second = row % 4, row >= 4
    start = jnp.where(second, 7919, 0) + seed
    a = residue(residue(residue(jnp.broadcast_to(index, shape)) * 40503) + start)
    a = residue(a * a)
    factor = 2 * (29989 * step % PRIME) % PRIME
    product = residue(a * jnp.where(kind == 1, a, factor))
    product = residue(product + jnp.where(kind == 1, 12345 - HALF_PRIME + PRIME, 0))
    return jnp.where(kind == 0, centred(a), fixed(product))


def by_second(index, step):
    shift = 29989 * step % PRIME
    b = residue(residue(index) * 29989)
    slope = residue(b * (2 * shift % PRIME))
    return [
        fixed(residue(2 * b)),
        fixed(residue(b * b)),
        fixed(residue(slope + shift * shift % PRIME)),
    ]


def tables_kernel(parts, half, where_ref, seeds_ref, first_ref, second_ref):
    core, col = where_ref[0], where_ref[1]
    index = lax.broadcasted_iota(jnp.int32, (1, first_ref.shape[1]), 1)
    first_ref[...] = by_first(index, seeds_ref[0], SUBLANES)
    sub = lax.broadcasted_iota(jnp.int32, (SUBLANES, LANES), 0)
    for s in range(parts):
        index = ((col ^ s) * 2 + core) * half + sub
        for i, value in enumerate(by_second(index, SUBLANES)):
            second_ref[s, i] = value


def tables(where, seeds, depth, parts, half):
    return pl.pallas_call(
        functools.partial(tables_kernel, parts, half),
        out_shape=[
            jax.ShapeDtypeStruct((8, depth), jnp.int32),
            jax.ShapeDtypeStruct((parts, 3, SUBLANES, LANES), jnp.int32),
        ],
        in_specs=[pl.BlockSpec(memory_space=pltpu.SMEM)] * 2,
        out_specs=[pl.BlockSpec(memory_space=pltpu.VMEM)] * 2,
        name="tables",
    )(where, seeds)


def limb_pair(value):
    rounded = value.astype(jnp.float32) * SCALE + FINE
    kept = (rounded + COARSE) - COARSE
    return (rounded - kept).astype(jnp.bfloat16), (kept - FINE_OFFSET).astype(jnp.bfloat16)


def join(products):
    low_p, high_p, low_q, high_q = products
    small = np.float32(1 / 256)
    p = low_p.astype(jnp.int32) + ((high_p * small).astype(jnp.int32) << 8)
    q = low_q.astype(jnp.int32) + ((high_q * small).astype(jnp.int32) << 8)
    return p + (q << 16)


def make_limbs(first_ref, second, start, width, lane, count, store):
    second = [jnp.concatenate([value] * (lane // LANES), axis=1) for value in second]
    for t in range(width // lane):
        at = pl.ds(pl.multiple_of(start + t * lane, lane), lane)
        for mix in range(2):
            a, square, slope = (first_ref[4 * mix + i : 4 * mix + i + 1, at] for i in range(3))
            value = a * second[0] + square + second[1]
            slope = slope + second[2]
            for k in range(count):
                low, high = limb_pair(value)
                store(2 * mix, k * SUBLANES, t * lane, low)
                store(2 * mix + 1, k * SUBLANES, t * lane, high)
                value = value + slope
                slope = slope + bend(SUBLANES)


def first_kernel(width, lane, own_ref, peer_ref, first_ref, second_ref, out_ref, even, odd):
    half = out_ref.shape[0]
    total = own_ref.shape[1] // width

    def make(step, limbs):
        def store(i, row, column, value):
            top = i * half + row
            limbs[top : top + SUBLANES, column : column + lane] = value

        second = [second_ref[i] for i in range(3)]
        make_limbs(first_ref, second, step * width, width, lane, half // SUBLANES, store)

    def use(step, limbs):
        at = pl.ds(pl.multiple_of(step * width, width), width)
        records = jnp.concatenate([own_ref[:, at], peer_ref[:, at]], axis=0)
        product = lax.dot_general(limbs[...], records, NT, preferred_element_type=jnp.float32)
        out_ref[...] += join([product[i * half : (i + 1) * half] for i in range(4)])

    out_ref[...] = jnp.zeros_like(out_ref)
    make(0, even)

    @pl.loop(0, total // 2 - 1)
    def _(i):
        use(2 * i, even)
        make(2 * i + 1, odd)
        use(2 * i + 1, odd)
        make(2 * i + 2, even)

    use(total - 2, even)
    make(total - 1, odd)
    use(total - 1, odd)


def first_hint(own, peer, by_column, by_n, s, half):
    rows, depth = own.shape
    width = min(1024, depth)
    lane = min(512, width)
    whole = pl.BlockSpec(memory_space=pltpu.VMEM)
    return pl.pallas_call(
        functools.partial(first_kernel, width, lane),
        grid=(1,),
        out_shape=jax.ShapeDtypeStruct((half, 2 * rows), jnp.int32),
        in_specs=[whole] * 3 + [pl.BlockSpec((None,) + by_n.shape[1:], lambda i: (s, 0, 0, 0))],
        out_specs=whole,
        scratch_shapes=[pltpu.VMEM((4 * half, width), jnp.bfloat16)] * 2,
        cost_estimate=pl.CostEstimate(
            flops=64 * half * depth * rows, bytes_accessed=4 * depth * rows, transcendentals=0
        ),
        name="first_hint",
    )(own, peer, by_column, by_n)


def rows_kernel(seeds_ref, place_ref, out_ref):
    out_ref[...] = by_first(place_ref[...], seeds_ref[1], SUBLANES)


def row_tables(place, seeds):
    return pl.pallas_call(
        rows_kernel,
        out_shape=jax.ShapeDtypeStruct((8, place.shape[1]), jnp.int32),
        in_specs=[
            pl.BlockSpec(memory_space=pltpu.SMEM),
            pl.BlockSpec(memory_space=pltpu.VMEM),
        ],
        name="row_tables",
    )(seeds, place)


def matrix_kernel(first_ref, *refs):
    out_ref = refs[-1]
    _, block, depth = out_ref.shape

    def store(i, row, column, value):
        out_ref[i, row : row + SUBLANES, column : column + value.shape[1]] = value

    sub = lax.broadcasted_iota(jnp.int32, (SUBLANES, LANES), 0)
    second = by_second(pl.program_id(0) * block + sub, SUBLANES)
    make_limbs(first_ref, second, 0, depth, min(512, depth), block // SUBLANES, store)


def second_matrix(by_row, t, depth, columns, after=None):
    block = min(256, columns)
    return pl.pallas_call(
        matrix_kernel,
        grid=(columns // block,),
        out_shape=jax.ShapeDtypeStruct((4, columns, depth), jnp.bfloat16),
        in_specs=[pl.BlockSpec((8, depth), lambda i: (0, t))]
        + ([] if after is None else [pl.BlockSpec(memory_space=pl.ANY)]),
        out_specs=pl.BlockSpec((4, block, depth), lambda i: (0, i, 0)),
        cost_estimate=pl.CostEstimate(
            flops=400 * 20 * depth * columns,
            bytes_accessed=8 * depth * columns,
            transcendentals=0,
        ),
        name="second_matrix",
    )(by_row, *([] if after is None else [after]))


def second_kernel(count, hint_refs, matrix_ref, total_ref, out_ref, digits):
    @pl.when(pl.program_id(0) == 0)
    def _():
        half, rows = hint_refs[0].shape[-2:]
        hints = [ref[i] for ref in hint_refs for i in range(ref.shape[0])]
        for s, hint in enumerate(hints):
            for place in range(4):
                byte = (lax.shift_right_logical(hint, jnp.int32(8 * place)) & 255) - 128
                digits[place * half : (place + 1) * half, s * rows : (s + 1) * rows] = byte.astype(
                    jnp.float32
                ).astype(jnp.bfloat16)

    half = out_ref.shape[1]
    total = join(
        [
            lax.dot_general(digits[...], matrix_ref[i], NT, preferred_element_type=jnp.float32)
            for i in range(4)
        ]
    )
    for place in range(4):
        term = total[place * half : (place + 1) * half]
        out_ref[place] = term if total_ref is None else total_ref[place] + term


def second_hint(hints, matrix, total=None):
    half, rows = hints[0].shape[1:]
    _, columns, depth = matrix.shape
    block = min(256, columns)
    out_spec = pl.BlockSpec((4, half, block), lambda i: (0, 0, i))
    count = len(hints)

    def kernel(*refs):
        previous = None if total is None else refs[count + 1]
        second_kernel(count, refs[:count], refs[count], previous, refs[-2], refs[-1])

    return pl.pallas_call(
        kernel,
        grid=(columns // block,),
        out_shape=jax.ShapeDtypeStruct((4, half, columns), jnp.int32),
        in_specs=[pl.BlockSpec(hint.shape, lambda i: (0, 0, 0)) for hint in hints]
        + [pl.BlockSpec((4, block, depth), lambda i: (0, i, 0))]
        + ([] if total is None else [out_spec]),
        out_specs=out_spec,
        scratch_shapes=[pltpu.VMEM((4 * half, depth), jnp.bfloat16)],
        input_output_aliases={} if total is None else {count + 1: 0},
        cost_estimate=pl.CostEstimate(
            flops=32 * half * depth * columns,
            bytes_accessed=8 * depth * columns + 32 * half * columns,
            transcendentals=0,
        ),
        name="second_hint",
    )(*hints, matrix, *([] if total is None else [total]))


def halves_kernel(_, value_ref, *refs):
    out_ref = refs[-1]
    value = value_ref[...]
    scale = np.float32(1 / 65536)
    out_ref[:, 0] = (value & 65535).astype(jnp.float32) * scale
    out_ref[:, 1] = lax.shift_right_logical(value, jnp.int32(16)).astype(jnp.float32) * scale


def write_halves(value, place, out=None):
    digits, half, columns = value.shape
    return pl.pallas_call(
        halves_kernel,
        grid_spec=pltpu.PrefetchScalarGridSpec(
            num_scalar_prefetch=1,
            grid=(digits,),
            in_specs=[pl.BlockSpec((1, half, columns), lambda i, place: (i, 0, 0))]
            + ([] if out is None else [pl.BlockSpec(memory_space=pl.ANY)]),
            out_specs=pl.BlockSpec((1, 2, half, columns), lambda i, place: (i, 0, place[0], 0)),
        ),
        out_shape=jax.ShapeDtypeStruct((digits, 2, 2 * half, columns), jnp.float32),
        input_output_aliases={} if out is None else {2: 0},
        name="write_halves",
    )(place, value, *([] if out is None else [out]))


def shift_by(value, axis, offset):
    return lax.ppermute(value, axis, [(i, i ^ offset) for i in range(lax.axis_size(axis))])


def on_device(ingest, row_order, matrix_seeds):
    row_size, col_size = lax.axis_size("row"), lax.axis_size("col")
    row, col = lax.axis_index("row"), lax.axis_index("col")
    core = row % 2
    rows, depth = ingest.shape
    half = N // col_size // 2

    peer = shift_by(ingest, "row", 1)
    order = row_order[0]
    block_rows = order.shape[0]
    k_index = lax.broadcasted_iota(jnp.int32, (block_rows, block_rows), 1)
    r_index = lax.broadcasted_iota(jnp.int32, (block_rows, block_rows), 0)
    place = jnp.sum(jnp.where(order[None, :] == r_index, k_index, 0), axis=1) + row * block_rows
    place = jnp.concatenate(
        [lax.dynamic_slice_in_dim(place, (col ^ s) * rows, rows) for s in range(col_size)]
    )
    place = jnp.stack([place, shift_by(place, "row", 1)])
    places = [place] + [shift_by(place, "row", 2 * t) for t in range(1, row_size // 2)]

    where = jnp.stack([core, col]).astype(jnp.int32)
    by_column, by_n = tables(where, matrix_seeds, depth, col_size, half)

    hints = [None] * col_size
    for s in reversed(range(col_size)):
        part = first_hint(ingest, peer, by_column, by_n, s, half)
        hints[s] = shift_by(part, "col", s) if s else part

    place = jnp.stack(places).reshape(row_size // 2, 2, col_size, rows).transpose(0, 2, 1, 3)
    by_row = row_tables(place.reshape(1, -1), matrix_seeds)

    cut = col_size // 2
    late, early = jnp.stack(hints[:cut]), jnp.stack(hints[cut:])
    total = None
    for t in range(row_size // 2):
        matrix = second_matrix(by_row, t, 2 * col_size * rows, N, total if t >= 4 else None)
        groups = [shift_by(late, "row", 2 * t), shift_by(early, "row", 2 * t)] if t else [late, early]
        total = second_hint(groups, matrix, total)

    other = shift_by(total, "row", 1)
    out = write_halves(total, core[None])
    return write_halves(other, 1 - core[None], out)


def solution(mesh):
    in_specs = (P(("row", "col"), None), P("row", None), P())
    out_specs = P(None, None, "col", None)
    return jax.shard_map(
        on_device, mesh=mesh, in_specs=in_specs, out_specs=out_specs, check_vma=False
    )
```

```python
import functools

import jax
import jax.numpy as jnp
import numpy as np
from jax import lax
from jax.experimental import pallas as pl
from jax.experimental.pallas import tpu as pltpu
from jax.sharding import PartitionSpec as P

N = 1024

PRIME = 46337
HALF_PRIME = PRIME // 2
WHOLE = (1 << 32) // PRIME
PART = (1 << 32) / PRIME - WHOLE
SCALE = np.float32(PRIME / 2.0**32)
FINE = np.float32(1.5 * 2.0**23)
INVERSE = np.float32(1 / PRIME)
OFFSET = 32896 - HALF_PRIME
COARSE = np.float32(1.5 * 2.0**31 - 1.5 * 2.0**23 - OFFSET)
FINE_OFFSET = np.float32(1.5 * 2.0**23 + OFFSET)
SUBLANES = 16
VMEM_LIMIT = 16 << 20
LANES = 128
NT = (((1,), (1,)), ((), ()))


def residue(value):
    value = value - (value.astype(jnp.float32) * INVERSE).astype(jnp.int32) * PRIME
    value = value + jnp.where(value < 0, PRIME, 0)
    return value - jnp.where(value >= PRIME, PRIME, 0)


def centred(value):
    return value - jnp.where(value > HALF_PRIME, PRIME, 0)


def fixed(value):
    value = centred(value)
    return value * WHOLE + jnp.round(value.astype(jnp.float32) * np.float32(PART)).astype(jnp.int32)


def bend(step):
    value = 2 * (29989 * step % PRIME) ** 2 % PRIME
    value = value - PRIME if value > HALF_PRIME else value
    return np.int32(round(value * 2**32 / PRIME))


def by_first(index, seed, step):
    rows = 8
    shape = (rows, index.shape[1])
    row = lax.broadcasted_iota(jnp.int32, shape, 0)
    kind, second = row % 4, row >= 4
    start = jnp.where(second, 7919, 0) + seed
    a = residue(residue(residue(jnp.broadcast_to(index, shape)) * 40503) + start)
    a = residue(a * a)
    factor = 2 * (29989 * step % PRIME) % PRIME
    product = residue(a * jnp.where(kind == 1, a, factor))
    product = residue(product + jnp.where(kind == 1, 12345 - HALF_PRIME + PRIME, 0))
    return jnp.where(kind == 0, centred(a), fixed(product))


def by_second(index, step):
    shift = 29989 * step % PRIME
    b = residue(residue(index) * 29989)
    slope = residue(b * (2 * shift % PRIME))
    return [
        fixed(residue(2 * b)),
        fixed(residue(b * b)),
        fixed(residue(slope + shift * shift % PRIME)),
    ]


def tables_kernel(parts, half, where_ref, seeds_ref, first_ref, second_ref):
    core, col = where_ref[0], where_ref[1]
    index = lax.broadcasted_iota(jnp.int32, (1, first_ref.shape[1]), 1)
    first_ref[...] = by_first(index, seeds_ref[0], SUBLANES)
    sub = lax.broadcasted_iota(jnp.int32, (SUBLANES, LANES), 0)
    for s in range(parts):
        index = ((col ^ s) * 2 + core) * half + sub
        for i, value in enumerate(by_second(index, SUBLANES)):
            second_ref[s, i] = value


def tables(where, seeds, depth, parts, half):
    return pl.pallas_call(
        functools.partial(tables_kernel, parts, half),
        out_shape=[
            jax.ShapeDtypeStruct((8, depth), jnp.int32),
            jax.ShapeDtypeStruct((parts, 3, SUBLANES, LANES), jnp.int32),
        ],
        in_specs=[pl.BlockSpec(memory_space=pltpu.SMEM)] * 2,
        out_specs=[pl.BlockSpec(memory_space=pltpu.VMEM)] * 2,
        compiler_params=pltpu.CompilerParams(vmem_limit_bytes=VMEM_LIMIT),
        name="tables",
    )(where, seeds)


def limb_pair(value):
    rounded = value.astype(jnp.float32) * SCALE + FINE
    kept = (rounded + COARSE) - COARSE
    return (rounded - kept).astype(jnp.bfloat16), (kept - FINE_OFFSET).astype(jnp.bfloat16)


def join(products):
    low_p, high_p, low_q, high_q = (product.astype(jnp.int32) for product in products)
    return low_p + (((low_q + (high_q << 8)) << 8) + high_p << 8)


def make_limbs(first_ref, second, start, width, lane, count, store):
    second = [jnp.concatenate([value] * (lane // LANES), axis=1) for value in second]
    for t in range(width // lane):
        at = pl.ds(pl.multiple_of(start + t * lane, lane), lane)
        for mix in range(2):
            a, square, slope = (first_ref[4 * mix + i : 4 * mix + i + 1, at] for i in range(3))
            value = a * second[0] + square + second[1]
            slope = slope + second[2]
            for k in range(count):
                low, high = limb_pair(value)
                store(2 * mix, k * SUBLANES, t * lane, low)
                store(2 * mix + 1, k * SUBLANES, t * lane, high)
                value = value + slope
                slope = slope + bend(SUBLANES)


def first_kernel(width, lane, own_ref, peer_ref, first_ref, second_ref, *refs):
    outs, even, odd = refs[:-2], refs[-2], refs[-1]
    half = outs[0].shape[0]
    total = own_ref.shape[1] // width
    small = jnp.bfloat16(1 / 256)

    def make(step, limbs):
        for s in range(len(outs)):

            def store(i, row, column, value):
                top = ((i % 2 * len(outs) + s) * 2 + i // 2) * half + row
                limbs[top : top + SUBLANES, column : column + lane] = value

            second = [second_ref[s, i] for i in range(3)]
            make_limbs(first_ref, second, step * width, width, lane, half // SUBLANES, store)

    def use(step, limbs):
        at = pl.ds(pl.multiple_of(step * width, width), width)
        records = jnp.concatenate([own_ref[:, at], peer_ref[:, at]], axis=0)
        middle = limbs.shape[0] // 2
        low = lax.dot_general(limbs[:middle], records, NT, preferred_element_type=jnp.float32)
        high = lax.dot_general(
            limbs[middle:], records * small, NT, preferred_element_type=jnp.float32
        )
        for s, out_ref in enumerate(outs):
            p, q = (slice((2 * s + i) * half, (2 * s + i + 1) * half) for i in range(2))
            out_ref[...] += join([low[p], high[p], low[q], high[q]])

    for out_ref in outs:
        out_ref[...] = jnp.zeros_like(out_ref)
    make(0, even)

    @pl.loop(0, total // 2 - 1)
    def _(i):
        use(2 * i, even)
        make(2 * i + 1, odd)
        use(2 * i + 1, odd)
        make(2 * i + 2, even)

    use(total - 2, even)
    make(total - 1, odd)
    use(total - 1, odd)


def first_hint(own, peer, by_column, by_n, s, count, half, width, lane):
    rows, depth = own.shape
    width = min(width, depth)
    lane = min(lane, width)
    whole = pl.BlockSpec(memory_space=pltpu.VMEM)
    return pl.pallas_call(
        functools.partial(first_kernel, width, lane),
        grid=(1,),
        out_shape=[jax.ShapeDtypeStruct((half, 2 * rows), jnp.int32)] * count,
        in_specs=[whole] * 3
        + [pl.BlockSpec((count,) + by_n.shape[1:], lambda i: (s // count, 0, 0, 0))],
        out_specs=[whole] * count,
        scratch_shapes=[pltpu.VMEM((4 * count * half, width), jnp.bfloat16)] * 2,
        compiler_params=pltpu.CompilerParams(vmem_limit_bytes=VMEM_LIMIT),
        cost_estimate=pl.CostEstimate(
            flops=64 * count * half * depth * rows,
            bytes_accessed=4 * depth * rows,
            transcendentals=0,
        ),
        name="first_hint",
    )(own, peer, by_column, by_n)


def rows_kernel(seeds_ref, place_ref, out_ref):
    out_ref[...] = by_first(place_ref[...], seeds_ref[1], SUBLANES)


def row_tables(place, seeds):
    return pl.pallas_call(
        rows_kernel,
        out_shape=jax.ShapeDtypeStruct((8, place.shape[1]), jnp.int32),
        in_specs=[
            pl.BlockSpec(memory_space=pltpu.SMEM),
            pl.BlockSpec(memory_space=pltpu.VMEM),
        ],
        compiler_params=pltpu.CompilerParams(vmem_limit_bytes=VMEM_LIMIT),
        name="row_tables",
    )(seeds, place)


def matrix_kernel(block, first_ref, *refs):
    out_ref = refs[-1]
    _, columns, depth = out_ref.shape
    lane = min(512, depth)
    sub = lax.broadcasted_iota(jnp.int32, (SUBLANES, LANES), 0)

    @pl.loop(0, columns // block)
    def _(i):
        start = pl.multiple_of(i * block, block)

        def store(i, row, column, value):
            out_ref[i, pl.ds(start + row, SUBLANES), column : column + lane] = value

        second = by_second(start + sub, SUBLANES)
        make_limbs(first_ref, second, 0, depth, lane, block // SUBLANES, store)


def second_matrix(by_row, t, depth, columns, after=()):
    block = min(256, columns)
    whole = pl.BlockSpec(memory_space=pltpu.VMEM)
    return pl.pallas_call(
        functools.partial(matrix_kernel, block),
        grid=(1,),
        out_shape=jax.ShapeDtypeStruct((4, columns, depth), jnp.bfloat16),
        in_specs=[pl.BlockSpec((8, depth), lambda i: (0, t))]
        + [pl.BlockSpec(memory_space=pl.ANY)] * len(after),
        out_specs=whole,
        compiler_params=pltpu.CompilerParams(vmem_limit_bytes=VMEM_LIMIT),
        cost_estimate=pl.CostEstimate(
            flops=2000 * depth * columns,
            bytes_accessed=8 * depth * columns,
            transcendentals=0,
        ),
        name="second_matrix",
    )(by_row, *after)


def second_kernel(block, hint_ref, matrix_ref, total_ref, out_ref, digits, small_digits):
    pieces, half, rows = hint_ref.shape
    for s in range(pieces):
        hint = hint_ref[s]
        for place in range(4):
            byte = (lax.shift_right_logical(hint, jnp.int32(8 * place)) & 255) - 128
            byte = byte.astype(jnp.float32).astype(jnp.bfloat16)
            at = (slice(place * half, (place + 1) * half), slice(s * rows, (s + 1) * rows))
            digits[at] = byte
            small_digits[at] = byte * jnp.bfloat16(1 / 256)

    @pl.loop(0, matrix_ref.shape[1] // block)
    def _(i):
        at = pl.ds(pl.multiple_of(i * block, block), block)
        total = join(
            [
                lax.dot_general(
                    [digits, small_digits][limb % 2][...],
                    matrix_ref[limb, at],
                    NT,
                    preferred_element_type=jnp.float32,
                )
                for limb in range(4)
            ]
        )
        for place in range(4):
            term = total[place * half : (place + 1) * half]
            out_ref[place, :, at] = term if total_ref is None else total_ref[place, :, at] + term


def second_hint(hint, matrix, total=None):
    half = hint.shape[1]
    _, columns, depth = matrix.shape
    block = min(256, columns)
    whole = pl.BlockSpec(memory_space=pltpu.VMEM)

    def kernel(*refs):
        previous = None if total is None else refs[2]
        second_kernel(block, *refs[:2], previous, *refs[-3:])

    return pl.pallas_call(
        kernel,
        out_shape=jax.ShapeDtypeStruct((4, half, columns), jnp.int32),
        in_specs=[whole] * (2 if total is None else 3),
        out_specs=whole,
        scratch_shapes=[pltpu.VMEM((4 * half, depth), jnp.bfloat16)] * 2,
        input_output_aliases={} if total is None else {2: 0},
        compiler_params=pltpu.CompilerParams(vmem_limit_bytes=VMEM_LIMIT),
        cost_estimate=pl.CostEstimate(
            flops=32 * half * depth * columns,
            bytes_accessed=8 * depth * columns + 32 * half * columns,
            transcendentals=0,
        ),
        name="second_hint",
    )(hint, matrix, *([] if total is None else [total]))


def halves_kernel(_, value_ref, *refs):
    out_ref = refs[-1]
    value = value_ref[...]
    scale = np.float32(1 / 65536)
    out_ref[:, 0] = (value & 65535).astype(jnp.float32) * scale
    out_ref[:, 1] = lax.shift_right_logical(value, jnp.int32(16)).astype(jnp.float32) * scale


def write_halves(value, place, out=None):
    digits, half, columns = value.shape
    return pl.pallas_call(
        halves_kernel,
        grid_spec=pltpu.PrefetchScalarGridSpec(
            num_scalar_prefetch=1,
            grid=(digits,),
            in_specs=[pl.BlockSpec((1, half, columns), lambda i, place: (i, 0, 0))]
            + ([] if out is None else [pl.BlockSpec(memory_space=pl.ANY)]),
            out_specs=pl.BlockSpec((1, 2, half, columns), lambda i, place: (i, 0, place[0], 0)),
        ),
        out_shape=jax.ShapeDtypeStruct((digits, 2, 2 * half, columns), jnp.float32),
        input_output_aliases={} if out is None else {2: 0},
        compiler_params=pltpu.CompilerParams(vmem_limit_bytes=VMEM_LIMIT),
        name="write_halves",
    )(place, value, *([] if out is None else [out]))


def shift_by(value, axis, offset):
    return lax.ppermute(value, axis, [(i, i ^ offset) for i in range(lax.axis_size(axis))])


def on_device(ingest, row_order, matrix_seeds):
    row_size, col_size = lax.axis_size("row"), lax.axis_size("col")
    row, col = lax.axis_index("row"), lax.axis_index("col")
    core = row % 2
    rows, depth = ingest.shape
    half = N // col_size // 2

    peer = shift_by(ingest, "row", 1)
    order = row_order[0]
    block_rows = order.shape[0]
    k_index = lax.broadcasted_iota(jnp.int32, (block_rows, block_rows), 1)
    r_index = lax.broadcasted_iota(jnp.int32, (block_rows, block_rows), 0)
    place = jnp.sum(jnp.where(order[None, :] == r_index, k_index, 0), axis=1) + row * block_rows
    place = jnp.concatenate(
        [lax.dynamic_slice_in_dim(place, (col ^ s) * rows, rows) for s in range(col_size)]
    )
    place = jnp.stack([place, shift_by(place, "row", 1)])
    places = [place] + [shift_by(place, "row", 2 * t) for t in range(1, row_size // 2)]

    where = jnp.stack([core, col]).astype(jnp.int32)
    by_column, by_n = tables(where, matrix_seeds, depth, col_size, half)

    hints = [None] * col_size
    count = 2
    for s in reversed(range(0, col_size, count)):
        parts = first_hint(ingest, peer, by_column, by_n, s, count, half, 1024, 512)
        for i, part in enumerate(parts):
            hints[s + i] = shift_by(part, "col", s + i) if s + i else part

    place = jnp.stack(places).reshape(row_size // 2, 2, col_size, rows).transpose(0, 2, 1, 3)
    by_row = row_tables(place.reshape(1, -1), matrix_seeds)

    stacked = jnp.stack(hints)
    total = None
    for t in range(row_size // 2):
        after = [hints[0]] if t < 4 else [total]
        matrix = second_matrix(by_row, t, 2 * col_size * rows, N, after)
        hint = shift_by(stacked, "row", 2 * t) if t else stacked
        total = second_hint(hint, matrix, total)

    other = shift_by(total, "row", 1)
    out = write_halves(total, core[None])
    return write_halves(other, 1 - core[None], out)


def solution(mesh):
    in_specs = (P(("row", "col"), None), P("row", None), P())
    out_specs = P(None, None, "col", None)
    return jax.shard_map(
        on_device, mesh=mesh, in_specs=in_specs, out_specs=out_specs, check_vma=False
    )
```

```python
import functools

import jax
import jax.numpy as jnp
import numpy as np
from jax import lax
from jax.experimental import pallas as pl
from jax.experimental.pallas import tpu as pltpu
from jax.sharding import PartitionSpec as P


N = 1024

PRIME = 46337
HALF_PRIME = PRIME // 2
WHOLE = (1 << 32) // PRIME
PART = (1 << 32) / PRIME - WHOLE
SCALE = np.float32(PRIME / 2.0**32)
FINE = np.float32(1.5 * 2.0**23)
INVERSE = np.float32(1 / PRIME)
OFFSET = 32896 - HALF_PRIME
COARSE = np.float32(1.5 * 2.0**31 - 1.5 * 2.0**23 - OFFSET)
FINE_OFFSET = np.float32(1.5 * 2.0**23 + OFFSET)
SUBLANES = 16
VMEM_LIMIT = 16 << 20
LANES = 128
NT = (((1,), (1,)), ((), ()))


def residue(value):
    value = value - (value.astype(jnp.float32) * INVERSE).astype(jnp.int32) * PRIME
    value = value + jnp.where(value < 0, PRIME, 0)
    return value - jnp.where(value >= PRIME, PRIME, 0)


def centred(value):
    return value - jnp.where(value > HALF_PRIME, PRIME, 0)


def fixed(value):
    value = centred(value)
    return value * WHOLE + jnp.round(value.astype(jnp.float32) * np.float32(PART)).astype(jnp.int32)


def bend(step):
    value = 2 * (29989 * step % PRIME) ** 2 % PRIME
    value = value - PRIME if value > HALF_PRIME else value
    return np.int32(round(value * 2**32 / PRIME))


def by_first(index, seed, step):
    rows = 8
    shape = (rows, index.shape[1])
    row = lax.broadcasted_iota(jnp.int32, shape, 0)
    kind, second = row % 4, row >= 4
    start = jnp.where(second, 7919, 0) + seed
    a = residue(residue(residue(jnp.broadcast_to(index, shape)) * 40503) + start)
    a = residue(a * a)
    factor = 2 * (29989 * step % PRIME) % PRIME
    product = residue(a * jnp.where(kind == 1, a, factor))
    product = residue(product + jnp.where(kind == 1, 12345 - HALF_PRIME + PRIME, 0))
    return jnp.where(kind == 0, centred(a), fixed(product))


def by_second(index, step):
    shift = 29989 * step % PRIME
    b = residue(residue(index) * 29989)
    slope = residue(b * (2 * shift % PRIME))
    return [
        fixed(residue(2 * b)),
        fixed(residue(b * b)),
        fixed(residue(slope + shift * shift % PRIME)),
    ]


def tables_kernel(half, block_rows, seeds_ref, column_ref, n_ref, row_ref):
    row, col = lax.axis_index("row"), lax.axis_index("col")
    index = lax.broadcasted_iota(jnp.int32, (1, column_ref.shape[1]), 1)
    column_ref[...] = by_first(index, seeds_ref[0], SUBLANES)
    pair_rows = 2 * block_rows
    for t in range(row_ref.shape[0]):
        index = (row // 2 ^ t) * pair_rows + lax.broadcasted_iota(jnp.int32, (1, pair_rows), 1)
        row_ref[t] = by_first(index, seeds_ref[1], SUBLANES)
    sub = lax.broadcasted_iota(jnp.int32, (SUBLANES, LANES), 0)
    for s in range(n_ref.shape[0]):
        index = ((col ^ s) * 2 + row % 2) * half + sub
        for i, value in enumerate(by_second(index, SUBLANES)):
            n_ref[s, i] = value


def tables(seeds, depth, parts, half, chips, block_rows):
    return pl.pallas_call(
        functools.partial(tables_kernel, half, block_rows),
        out_shape=[
            jax.ShapeDtypeStruct((8, depth), jnp.int32),
            jax.ShapeDtypeStruct((parts, 3, SUBLANES, LANES), jnp.int32),
            jax.ShapeDtypeStruct((chips, 8, 2 * block_rows), jnp.int32),
        ],
        in_specs=[pl.BlockSpec(memory_space=pltpu.SMEM)],
        out_specs=[pl.BlockSpec(memory_space=pltpu.VMEM)] * 3,
        compiler_params=pltpu.CompilerParams(vmem_limit_bytes=VMEM_LIMIT),
        name="tables",
    )(seeds)


def limb_pair(value):
    rounded = value.astype(jnp.float32) * SCALE + FINE
    kept = (rounded + COARSE) - COARSE
    return (rounded - kept).astype(jnp.bfloat16), (kept - FINE_OFFSET).astype(jnp.bfloat16)


def join(products):
    low_p, high_p, low_q, high_q = (whole_number(product) for product in products)
    return low_p + (((low_q + (high_q << 8)) << 8) + high_p << 8)


def make_limbs(first_ref, second, start, width, lane, count, store):
    second = [jnp.concatenate([value] * (lane // LANES), axis=1) for value in second]
    for t in range(width // lane):
        at = pl.ds(pl.multiple_of(start + t * lane, lane), lane)
        for mix in range(2):
            a, square, slope = (first_ref[4 * mix + i : 4 * mix + i + 1, at] for i in range(3))
            value = a * second[0] + square + second[1]
            slope = slope + second[2]
            for k in range(count):
                low, high = limb_pair(value)
                store(2 * mix, k * SUBLANES, t * lane, low)
                store(2 * mix + 1, k * SUBLANES, t * lane, high)
                value = value + slope
                slope = slope + bend(SUBLANES)


def first_kernel(width, lane, own_ref, peer_ref, first_ref, second_ref, *refs):
    outs, even, odd = refs[:-2], refs[-2], refs[-1]
    half = outs[0].shape[0]
    total = own_ref.shape[1] // width
    small = jnp.bfloat16(1 / 256)

    def make(step, limbs):
        for s in range(len(outs)):

            def store(i, row, column, value):
                top = ((i % 2 * len(outs) + s) * 2 + i // 2) * half + row
                limbs[top : top + SUBLANES, column : column + lane] = value

            second = [second_ref[s, i] for i in range(3)]
            make_limbs(first_ref, second, step * width, width, lane, half // SUBLANES, store)

    def use(step, limbs):
        at = pl.ds(pl.multiple_of(step * width, width), width)
        records = jnp.concatenate([own_ref[:, at], peer_ref[:, at]], axis=0)
        middle = limbs.shape[0] // 2
        low = lax.dot_general(limbs[:middle], records, NT, preferred_element_type=jnp.float32)
        high = lax.dot_general(
            limbs[middle:], records * small, NT, preferred_element_type=jnp.float32
        )
        for s, out_ref in enumerate(outs):
            p, q = (slice((2 * s + i) * half, (2 * s + i + 1) * half) for i in range(2))
            out_ref[...] += join([low[p], high[p], low[q], high[q]])

    for out_ref in outs:
        out_ref[...] = jnp.zeros_like(out_ref)
    make(0, even)

    @pl.loop(0, total // 2 - 1)
    def _(i):
        use(2 * i, even)
        make(2 * i + 1, odd)
        use(2 * i + 1, odd)
        make(2 * i + 2, even)

    use(total - 2, even)
    make(total - 1, odd)
    use(total - 1, odd)


def first_hint(own, peer, by_column, by_n, s, count, half, width, lane):
    rows, depth = own.shape
    width = min(width, depth)
    lane = min(lane, width)
    whole = pl.BlockSpec(memory_space=pltpu.VMEM)
    return pl.pallas_call(
        functools.partial(first_kernel, width, lane),
        grid=(1,),
        out_shape=[jax.ShapeDtypeStruct((half, 2 * rows), jnp.int32)] * count,
        in_specs=[whole] * 3
        + [pl.BlockSpec((count,) + by_n.shape[1:], lambda i: (s // count, 0, 0, 0))],
        out_specs=[whole] * count,
        scratch_shapes=[pltpu.VMEM((4 * count * half, width), jnp.bfloat16)] * 2,
        compiler_params=pltpu.CompilerParams(vmem_limit_bytes=VMEM_LIMIT),
        cost_estimate=pl.CostEstimate(
            flops=64 * count * half * depth * rows,
            bytes_accessed=4 * depth * rows,
            transcendentals=0,
        ),
        name="first_hint",
    )(own, peer, by_column, by_n)


def byte_digits(hint, place):
    byte = (lax.shift_right_logical(hint, jnp.int32(8 * place)) & 255) - 128
    return byte.astype(jnp.float32).astype(jnp.bfloat16)


def whole_number(value):
    return jnp.round(value).astype(jnp.int32)


def sort_kernel(pieces, *refs):
    hints, (own_ref, peer_ref, out_ref, digits, select) = refs[:pieces], refs[pieces:]
    core, col = lax.axis_index("row") % 2, lax.axis_index("col")
    half, rows = hints[0].shape
    block_rows = own_ref.shape[1]
    slice_rows = rows // 2
    for s, hint_ref in enumerate(hints):
        hint = hint_ref[...]
        for place in range(4):
            at = (slice(place * half, (place + 1) * half), slice(s * rows, (s + 1) * rows))
            digits[at] = byte_digits(hint, place)
    orders = [own_ref[...], peer_ref[...] + block_rows]
    swapped = core == 1
    target = jnp.concatenate(
        [
            jnp.where(swapped, orders[1], orders[0]),
            jnp.where(swapped, orders[0], orders[1]),
        ],
        axis=1,
    )
    for s in range(pieces):
        for e in range(2):
            start = e * block_rows + (col ^ s) * slice_rows
            row = start + lax.broadcasted_iota(jnp.int32, (slice_rows, 2 * block_rows), 0)
            top = s * rows + e * slice_rows
            select[top : top + slice_rows, :] = jnp.where(row == target, 1.0, 0.0).astype(
                jnp.bfloat16
            )
    hint = None
    for place in range(4):
        moved = jnp.dot(
            digits[place * half : (place + 1) * half],
            select[...],
            preferred_element_type=jnp.float32,
        )
        term = (whole_number(moved) + 128) << (8 * place)
        hint = term if hint is None else hint + term
    out_ref[...] = hint


def sort_rows(hints, own_order, peer_order):
    half, _ = hints[0].shape
    total = 2 * own_order.shape[1]
    whole = pl.BlockSpec(memory_space=pltpu.VMEM)
    return pl.pallas_call(
        functools.partial(sort_kernel, len(hints)),
        out_shape=jax.ShapeDtypeStruct((half, total), jnp.int32),
        in_specs=[whole] * (len(hints) + 2),
        out_specs=whole,
        scratch_shapes=[
            pltpu.VMEM((4 * half, total), jnp.bfloat16),
            pltpu.VMEM((total, total), jnp.bfloat16),
        ],
        compiler_params=pltpu.CompilerParams(vmem_limit_bytes=VMEM_LIMIT),
        name="sort_rows",
    )(*hints, own_order, peer_order)


def matrix_kernel(block, first_ref, *refs):
    out_ref = refs[-1]
    count, _, depth = first_ref.shape
    columns = out_ref.shape[1]
    lane = min(512, depth)
    sub = lax.broadcasted_iota(jnp.int32, (SUBLANES, LANES), 0)

    @pl.loop(0, columns // block)
    def _(i):
        start = pl.multiple_of(i * block, block)
        second = by_second(start + sub, SUBLANES)
        for t in range(count):

            def store(i, row, column, value):
                at = slice(t * depth + column, t * depth + column + lane)
                out_ref[i, pl.ds(start + row, SUBLANES), at] = value

            make_limbs(first_ref.at[t], second, 0, depth, lane, block // SUBLANES, store)


def second_matrix(by_row, group, count, columns, after=()):
    _, quantities, depth = by_row.shape
    block = min(128, columns)
    whole = pl.BlockSpec(memory_space=pltpu.VMEM)
    return pl.pallas_call(
        functools.partial(matrix_kernel, block),
        grid=(1,),
        out_shape=jax.ShapeDtypeStruct((4, columns, count * depth), jnp.bfloat16),
        in_specs=[pl.BlockSpec((count, quantities, depth), lambda i: (group, 0, 0))]
        + [pl.BlockSpec(memory_space=pl.ANY)] * len(after),
        out_specs=whole,
        compiler_params=pltpu.CompilerParams(vmem_limit_bytes=VMEM_LIMIT),
        cost_estimate=pl.CostEstimate(
            flops=2000 * count * depth * columns,
            bytes_accessed=8 * count * depth * columns,
            transcendentals=0,
        ),
        name="second_matrix",
    )(by_row, *after)


def second_kernel(block, places, hints, matrix_ref, totals, outs, digits, small_digits):
    half, rows = hints[0].shape
    for t, hint_ref in enumerate(hints):
        hint = hint_ref[...]
        for i, place in enumerate(places):
            byte = byte_digits(hint, place)
            at = (slice(i * half, (i + 1) * half), slice(t * rows, (t + 1) * rows))
            digits[at] = byte
            small_digits[at] = byte * jnp.bfloat16(1 / 256)

    per_out = len(places) // len(outs)
    for start in range(0, matrix_ref.shape[1], block):
        at = slice(start, start + block)
        total = join(
            [
                lax.dot_general(
                    [digits, small_digits][limb % 2][...],
                    matrix_ref[limb, at],
                    NT,
                    preferred_element_type=jnp.float32,
                )
                for limb in range(4)
            ]
        )
        for i in range(len(places)):
            term = total[i * half : (i + 1) * half]
            k, j = i // per_out, i % per_out
            outs[k][j, :, at] = totals[k][j, :, at] + term if totals else term


def second_hint(hints, matrix, places, count, totals=()):
    half = hints[0].shape[0]
    _, columns, depth = matrix.shape
    block = min(256, columns)
    whole = pl.BlockSpec(memory_space=pltpu.VMEM)
    inputs = len(hints) + 1

    def kernel(*refs):
        outs = refs[inputs + len(totals) : -2]
        previous = refs[inputs : inputs + len(totals)]
        second_kernel(block, places, refs[: inputs - 1], refs[inputs - 1], previous, outs, *refs[-2:])

    shape = jax.ShapeDtypeStruct((len(places) // count, half, columns), jnp.int32)
    return pl.pallas_call(
        kernel,
        out_shape=[shape] * count,
        in_specs=[whole] * (inputs + len(totals)),
        out_specs=[whole] * count,
        scratch_shapes=[pltpu.VMEM((len(places) * half, depth), jnp.bfloat16)] * 2,
        input_output_aliases={inputs + i: i for i in range(len(totals))},
        compiler_params=pltpu.CompilerParams(vmem_limit_bytes=VMEM_LIMIT),
        cost_estimate=pl.CostEstimate(
            flops=8 * len(places) * half * depth * columns,
            bytes_accessed=8 * depth * columns + 8 * len(places) * half * columns,
            transcendentals=0,
        ),
        name="second_hint",
    )(*hints, matrix, *totals)


def halves_kernel(first, flip, value_ref, *refs):
    out_ref, low, high, sems = refs[-4:]
    digits, half, _ = value_ref.shape
    core = lax.axis_index("row") % 2
    start = pl.multiple_of((1 - core if flip else core) * half, half)
    rows = low.shape[2]
    scale = np.float32(1 / 65536)
    copies = []
    for i in range(digits):
        for j in range(half // rows):
            value = value_ref[i, j * rows : (j + 1) * rows]
            low[i, j] = (value & 65535).astype(jnp.float32) * scale
            high[i, j] = lax.shift_right_logical(value, jnp.int32(16)).astype(jnp.float32) * scale
            for k, source in enumerate((low, high)):
                target = out_ref.at[first + i, k, pl.ds(start + j * rows, rows)]
                copies.append(pltpu.make_async_copy(source.at[i, j], target, sems.at[i, j, k]))
                copies[-1].start()
    for copy in copies:
        copy.wait()


def write_halves(value, flip, first, out=None):
    digits, half, columns = value.shape
    rows = max(half // 2, 8)
    cuts = half // rows
    anywhere = pl.BlockSpec(memory_space=pl.ANY)
    return pl.pallas_call(
        functools.partial(halves_kernel, first, flip),
        in_specs=[pl.BlockSpec(memory_space=pltpu.VMEM)] + [anywhere] * (out is not None),
        out_specs=anywhere,
        out_shape=jax.ShapeDtypeStruct((4, 2, 2 * half, columns), jnp.float32),
        scratch_shapes=[pltpu.VMEM((digits, cuts, rows, columns), jnp.float32)] * 2
        + [pltpu.SemaphoreType.DMA((digits, cuts, 2))],
        input_output_aliases={} if out is None else {1: 0},
        compiler_params=pltpu.CompilerParams(vmem_limit_bytes=VMEM_LIMIT),
        name="write_halves",
    )(value, *([] if out is None else [out]))


def shift_by(value, axis, offset):
    return lax.ppermute(value, axis, [(i, i ^ offset) for i in range(lax.axis_size(axis))])


def on_device(ingest, row_order, matrix_seeds):
    row_size, col_size = lax.axis_size("row"), lax.axis_size("col")
    rows, depth = ingest.shape
    half = N // col_size // 2
    chips = row_size // 2
    pair_rows = 2 * col_size * rows

    peer = shift_by(ingest, "row", 1)
    peer_order = shift_by(row_order, "row", 1)
    by_column, by_n, by_row = tables(
        matrix_seeds, depth, col_size, half, chips, row_order.shape[1]
    )

    hints = [None] * col_size
    count = 2
    for s in reversed(range(0, col_size, count)):
        parts = first_hint(ingest, peer, by_column, by_n, s, count, half, 1024, 512)
        for i, part in enumerate(parts):
            hints[s + i] = shift_by(part, "col", s + i) if s + i else part
    hint = sort_rows(hints, row_order, peer_order)
    sources = [hint]
    for t in range(1, chips):
        sources.append(shift_by(hint, "row", 2 * t))

    count = max(1, min(chips, 1024 // pair_rows))
    totals = ()
    for group in range(chips // count):
        after = [] if group < 2 else [totals[0]]
        matrix = second_matrix(by_row, group, count, N, after)
        some = sources[group * count : (group + 1) * count]
        if group < chips // count - 1:
            totals = second_hint(some, matrix, (0, 1, 2, 3), 2, totals)
        else:
            totals = [
                second_hint(some, matrix, (2 * i, 2 * i + 1), 1, totals[i : i + 1])[0]
                for i in range(2)
            ]

    others = [shift_by(total, "row", 1) for total in totals]
    out = None
    for flip, values in enumerate((totals, others)):
        for i, value in enumerate(values):
            out = write_halves(value, flip, 2 * i, out)
    return out


def solution(mesh):
    in_specs = (P(("row", "col"), None), P("row", None), P())
    out_specs = P(None, None, "col", None)
    return jax.shard_map(
        on_device, mesh=mesh, in_specs=in_specs, out_specs=out_specs, check_vma=False
    )
```

```python
import functools

import jax
import jax.numpy as jnp
import numpy as np
from jax import lax
from jax.experimental import pallas as pl
from jax.experimental.pallas import tpu as pltpu
from jax.sharding import PartitionSpec as P


N = 1024

PRIME = 46337
HALF_PRIME = PRIME // 2
WHOLE = (1 << 32) // PRIME
PART = (1 << 32) / PRIME - WHOLE
SCALE = np.float32(PRIME / 2.0**32)
FINE = np.float32(1.5 * 2.0**23)
INVERSE = np.float32(1 / PRIME)
OFFSET = 32896 - HALF_PRIME
COARSE = np.float32(1.5 * 2.0**31 - 1.5 * 2.0**23 - OFFSET)
FINE_OFFSET = np.float32(1.5 * 2.0**23 + OFFSET)
SUBLANES = 16
VMEM_LIMIT = 16 << 20
LANES = 128
NT = (((1,), (1,)), ((), ()))


def residue(value):
    value = value - (value.astype(jnp.float32) * INVERSE).astype(jnp.int32) * PRIME
    value = value + jnp.where(value < 0, PRIME, 0)
    return value - jnp.where(value >= PRIME, PRIME, 0)


def centred(value):
    return value - jnp.where(value > HALF_PRIME, PRIME, 0)


def fixed(value):
    value = centred(value)
    return value * WHOLE + jnp.round(value.astype(jnp.float32) * np.float32(PART)).astype(jnp.int32)


def bend(step):
    value = 2 * (29989 * step % PRIME) ** 2 % PRIME
    value = value - PRIME if value > HALF_PRIME else value
    return np.int32(round(value * 2**32 / PRIME))


def by_first(index, seed, step):
    rows = 8
    shape = (rows, index.shape[1])
    row = lax.broadcasted_iota(jnp.int32, shape, 0)
    kind, second = row % 4, row >= 4
    start = jnp.where(second, 7919, 0) + seed
    a = residue(residue(residue(jnp.broadcast_to(index, shape)) * 40503) + start)
    a = residue(a * a)
    factor = 2 * (29989 * step % PRIME) % PRIME
    product = residue(a * jnp.where(kind == 1, a, factor))
    product = residue(product + jnp.where(kind == 1, 12345 - HALF_PRIME + PRIME, 0))
    return jnp.where(kind == 0, centred(a), fixed(product))


def by_second(index, step):
    shift = 29989 * step % PRIME
    b = residue(residue(index) * 29989)
    slope = residue(b * (2 * shift % PRIME))
    return [
        fixed(residue(2 * b)),
        fixed(residue(b * b)),
        fixed(residue(slope + shift * shift % PRIME)),
    ]


def tables_kernel(half, block_rows, seeds_ref, column_ref, n_ref, row_ref):
    row, col = lax.axis_index("row"), lax.axis_index("col")
    index = lax.broadcasted_iota(jnp.int32, (1, column_ref.shape[1]), 1)
    column_ref[...] = by_first(index, seeds_ref[0], SUBLANES)
    pair_rows = 2 * block_rows
    for t in range(row_ref.shape[0]):
        index = (row // 2 ^ t) * pair_rows + lax.broadcasted_iota(jnp.int32, (1, pair_rows), 1)
        row_ref[t] = by_first(index, seeds_ref[1], SUBLANES)
    sub = lax.broadcasted_iota(jnp.int32, (SUBLANES, LANES), 0)
    for s in range(n_ref.shape[0]):
        index = ((col ^ s) * 2 + row % 2) * half + sub
        for i, value in enumerate(by_second(index, SUBLANES)):
            n_ref[s, i] = value


def tables(seeds, depth, parts, half, chips, block_rows):
    return pl.pallas_call(
        functools.partial(tables_kernel, half, block_rows),
        out_shape=[
            jax.ShapeDtypeStruct((8, depth), jnp.int32),
            jax.ShapeDtypeStruct((parts, 3, SUBLANES, LANES), jnp.int32),
            jax.ShapeDtypeStruct((chips, 8, 2 * block_rows), jnp.int32),
        ],
        in_specs=[pl.BlockSpec(memory_space=pltpu.SMEM)],
        out_specs=[pl.BlockSpec(memory_space=pltpu.VMEM)] * 3,
        compiler_params=pltpu.CompilerParams(vmem_limit_bytes=VMEM_LIMIT),
        name="tables",
    )(seeds)


def limb_pair(value):
    rounded = value.astype(jnp.float32) * SCALE + FINE
    kept = (rounded + COARSE) - COARSE
    return (rounded - kept).astype(jnp.bfloat16), (kept - FINE_OFFSET).astype(jnp.bfloat16)


def join(products):
    low_p, high_p, low_q, high_q = (whole_number(product) for product in products)
    return low_p + (((low_q + (high_q << 8)) << 8) + high_p << 8)


def make_limbs(first_ref, second, start, width, lane, count, store):
    second = [jnp.concatenate([value] * (lane // LANES), axis=1) for value in second]
    for t in range(width // lane):
        at = pl.ds(pl.multiple_of(start + t * lane, lane), lane)
        for mix in range(2):
            a, square, slope = (first_ref[4 * mix + i : 4 * mix + i + 1, at] for i in range(3))
            value = a * second[0] + square + second[1]
            slope = slope + second[2]
            for k in range(count):
                low, high = limb_pair(value)
                store(2 * mix, k * SUBLANES, t * lane, low)
                store(2 * mix + 1, k * SUBLANES, t * lane, high)
                value = value + slope
                slope = slope + bend(SUBLANES)


def first_kernel(offset, width, lane, own_ref, peer_ref, first_ref, second_ref, *refs):
    outs, even, odd = refs[:-2], refs[-2], refs[-1]
    half = outs[0].shape[0]
    total = own_ref.shape[1] // width
    small = jnp.bfloat16(1 / 256)

    def make(step, limbs):
        for s in range(len(outs)):

            def store(i, row, column, value):
                top = ((i % 2 * len(outs) + s) * 2 + i // 2) * half + row
                limbs[top : top + SUBLANES, column : column + lane] = value

            second = [second_ref[offset + s, i] for i in range(3)]
            make_limbs(first_ref, second, step * width, width, lane, half // SUBLANES, store)

    def use(step, limbs):
        at = pl.ds(pl.multiple_of(step * width, width), width)
        records = jnp.concatenate([own_ref[:, at], peer_ref[:, at]], axis=0)
        middle = limbs.shape[0] // 2
        low = lax.dot_general(limbs[:middle], records, NT, preferred_element_type=jnp.float32)
        high = lax.dot_general(
            limbs[middle:], records * small, NT, preferred_element_type=jnp.float32
        )
        for s, out_ref in enumerate(outs):
            p, q = (slice((2 * s + i) * half, (2 * s + i + 1) * half) for i in range(2))
            out_ref[...] += join([low[p], high[p], low[q], high[q]])

    for out_ref in outs:
        out_ref[...] = jnp.zeros_like(out_ref)
    make(0, even)

    @pl.loop(0, total // 2 - 1)
    def _(i):
        use(2 * i, even)
        make(2 * i + 1, odd)
        use(2 * i + 1, odd)
        make(2 * i + 2, even)

    use(total - 2, even)
    make(total - 1, odd)
    use(total - 1, odd)


def first_hint(own, peer, by_column, by_n, s, count, half, width, lane):
    rows, depth = own.shape
    width = min(width, depth)
    lane = min(lane, width)
    whole = pl.BlockSpec(memory_space=pltpu.VMEM)
    return pl.pallas_call(
        functools.partial(first_kernel, s, width, lane),
        out_shape=[jax.ShapeDtypeStruct((half, 2 * rows), jnp.int32)] * count,
        in_specs=[whole] * 4,
        out_specs=[whole] * count,
        scratch_shapes=[pltpu.VMEM((4 * count * half, width), jnp.bfloat16)] * 2,
        compiler_params=pltpu.CompilerParams(vmem_limit_bytes=VMEM_LIMIT),
        cost_estimate=pl.CostEstimate(
            flops=64 * count * half * depth * rows,
            bytes_accessed=4 * depth * rows,
            transcendentals=0,
        ),
        name="first_hint",
    )(own, peer, by_column, by_n)


def byte_digits(hint, place):
    byte = (lax.shift_right_logical(hint, jnp.int32(8 * place)) & 255) - 128
    return byte.astype(jnp.float32).astype(jnp.bfloat16)


def whole_number(value):
    return jnp.round(value).astype(jnp.int32)


def sort_kernel(pieces, *refs):
    hints, (own_ref, peer_ref, out_ref, digits, select) = refs[:pieces], refs[pieces:]
    core, col = lax.axis_index("row") % 2, lax.axis_index("col")
    half, rows = hints[0].shape
    block_rows = own_ref.shape[1]
    slice_rows = rows // 2
    for s, hint_ref in enumerate(hints):
        hint = hint_ref[...]
        for place in range(4):
            at = (slice(place * half, (place + 1) * half), slice(s * rows, (s + 1) * rows))
            digits[at] = byte_digits(hint, place)
    orders = [own_ref[...], peer_ref[...] + block_rows]
    swapped = core == 1
    target = jnp.concatenate(
        [
            jnp.where(swapped, orders[1], orders[0]),
            jnp.where(swapped, orders[0], orders[1]),
        ],
        axis=1,
    )
    for s in range(pieces):
        for e in range(2):
            start = e * block_rows + (col ^ s) * slice_rows
            row = start + lax.broadcasted_iota(jnp.int32, (slice_rows, 2 * block_rows), 0)
            top = s * rows + e * slice_rows
            select[top : top + slice_rows, :] = jnp.where(row == target, 1.0, 0.0).astype(
                jnp.bfloat16
            )
    hint = None
    for place in range(4):
        moved = jnp.dot(
            digits[place * half : (place + 1) * half],
            select[...],
            preferred_element_type=jnp.float32,
        )
        term = (whole_number(moved) + 128) << (8 * place)
        hint = term if hint is None else hint + term
    out_ref[...] = hint


def sort_rows(hints, own_order, peer_order):
    half, _ = hints[0].shape
    total = 2 * own_order.shape[1]
    whole = pl.BlockSpec(memory_space=pltpu.VMEM)
    return pl.pallas_call(
        functools.partial(sort_kernel, len(hints)),
        out_shape=jax.ShapeDtypeStruct((half, total), jnp.int32),
        in_specs=[whole] * (len(hints) + 2),
        out_specs=whole,
        scratch_shapes=[
            pltpu.VMEM((4 * half, total), jnp.bfloat16),
            pltpu.VMEM((total, total), jnp.bfloat16),
        ],
        compiler_params=pltpu.CompilerParams(vmem_limit_bytes=VMEM_LIMIT),
        name="sort_rows",
    )(*hints, own_order, peer_order)


def matrix_kernel(block, first_ref, *refs):
    out_ref = refs[-1]
    count, _, depth = first_ref.shape
    columns = out_ref.shape[1]
    lane = min(512, depth)
    sub = lax.broadcasted_iota(jnp.int32, (SUBLANES, LANES), 0)

    @pl.loop(0, columns // block)
    def _(i):
        start = pl.multiple_of(i * block, block)
        second = by_second(start + sub, SUBLANES)
        for t in range(count):

            def store(i, row, column, value):
                at = slice(t * depth + column, t * depth + column + lane)
                out_ref[i, pl.ds(start + row, SUBLANES), at] = value

            make_limbs(first_ref.at[t], second, 0, depth, lane, block // SUBLANES, store)


def second_matrix(by_row, group, count, columns, after=()):
    _, quantities, depth = by_row.shape
    block = min(128, columns)
    whole = pl.BlockSpec(memory_space=pltpu.VMEM)
    return pl.pallas_call(
        functools.partial(matrix_kernel, block),
        grid=(1,),
        out_shape=jax.ShapeDtypeStruct((4, columns, count * depth), jnp.bfloat16),
        in_specs=[pl.BlockSpec((count, quantities, depth), lambda i: (group, 0, 0))]
        + [pl.BlockSpec(memory_space=pl.ANY)] * len(after),
        out_specs=whole,
        compiler_params=pltpu.CompilerParams(vmem_limit_bytes=VMEM_LIMIT),
        cost_estimate=pl.CostEstimate(
            flops=2000 * count * depth * columns,
            bytes_accessed=8 * count * depth * columns,
            transcendentals=0,
        ),
        name="second_matrix",
    )(by_row, *after)


def second_kernel(block, first, count, has_total, has_next, *refs):
    refs = list(refs)
    hint_ref, matrix_ref = refs[:2]
    total_ref = refs[2] if has_total else None
    next_ref, next_matrix_ref = (refs[2 + has_total], refs[-3]) if has_next else (None, None)
    out_ref, digits, small_digits = refs[-4 if has_next else -3], refs[-2], refs[-1]
    half = hint_ref.shape[0]
    depth = matrix_ref.shape[2]
    hint = hint_ref[...]
    for place in range(4):
        byte = byte_digits(hint, place)
        digits[place * half : (place + 1) * half] = byte
        small_digits[place * half : (place + 1) * half] = byte * jnp.bfloat16(1 / 256)
    sub = lax.broadcasted_iota(jnp.int32, (SUBLANES, LANES), 0)
    lane = min(512, depth)

    for start in range(0, count, block):
        at = slice(first + start, first + start + block)
        total = join(
            [
                lax.dot_general(
                    [digits, small_digits][limb % 2][...],
                    matrix_ref[limb, at],
                    NT,
                    preferred_element_type=jnp.float32,
                )
                for limb in range(4)
            ]
        )
        for place in range(4):
            term = total[place * half : (place + 1) * half]
            out = slice(start, start + block)
            out_ref[place, :, out] = term if total_ref is None else total_ref[place, :, at] + term
        if has_next:

            def store(i, row, column, value, start=start):
                top = start + row
                next_matrix_ref[i, top : top + SUBLANES, column : column + lane] = value

            second = by_second(start + sub, SUBLANES)
            make_limbs(next_ref, second, 0, depth, lane, block // SUBLANES, store)


def second_hint(hint, matrix, first, count, total=None, by_row=None, t=0):
    half = hint.shape[0]
    depth = matrix.shape[2]
    has_total, has_next = total is not None, by_row is not None
    whole = pl.BlockSpec(memory_space=pltpu.VMEM)
    row_spec = pl.BlockSpec((None,) + by_row.shape[1:], lambda i: (t, 0, 0)) if has_next else None
    return pl.pallas_call(
        functools.partial(second_kernel, min(256, count), first, count, has_total, has_next),
        grid=(1,),
        out_shape=[jax.ShapeDtypeStruct((4, half, count), jnp.int32)]
        + [jax.ShapeDtypeStruct(matrix.shape, matrix.dtype)] * has_next,
        in_specs=[whole] * (2 + has_total) + [row_spec] * has_next,
        out_specs=[whole] * (1 + has_next),
        scratch_shapes=[pltpu.VMEM((4 * half, depth), jnp.bfloat16)] * 2,
        compiler_params=pltpu.CompilerParams(vmem_limit_bytes=VMEM_LIMIT),
        cost_estimate=pl.CostEstimate(
            flops=32 * half * depth * count,
            bytes_accessed=8 * depth * count + 32 * half * count,
            transcendentals=0,
        ),
        name="second_hint",
    )(hint, matrix, *([total] if has_total else []), *([by_row] if has_next else []))


def halves_kernel(first, flip, value_ref, *refs):
    out_ref, low, high, sems = refs[-4:]
    digits, half, columns = value_ref.shape
    core = lax.axis_index("row") % 2
    start = pl.multiple_of((1 - core if flip else core) * half, half)
    scale = np.float32(1 / 65536)
    copies = []
    for i in range(digits):
        value = value_ref[i]
        low[i] = (value & 65535).astype(jnp.float32) * scale
        high[i] = lax.shift_right_logical(value, jnp.int32(16)).astype(jnp.float32) * scale
        for k, source in enumerate((low, high)):
            target = out_ref.at[i, k, pl.ds(start, half), pl.ds(first, columns)]
            copies.append(pltpu.make_async_copy(source.at[i], target, sems.at[i, k]))
            copies[-1].start()
    for copy in copies:
        copy.wait()


def write_halves(value, flip, first, columns, out=None):
    digits, half, some = value.shape
    anywhere = pl.BlockSpec(memory_space=pl.ANY)
    return pl.pallas_call(
        functools.partial(halves_kernel, first, flip),
        in_specs=[pl.BlockSpec(memory_space=pltpu.VMEM)] + [anywhere] * (out is not None),
        out_specs=anywhere,
        out_shape=jax.ShapeDtypeStruct((digits, 2, 2 * half, columns), jnp.float32),
        scratch_shapes=[pltpu.VMEM((digits, half, some), jnp.float32)] * 2
        + [pltpu.SemaphoreType.DMA((digits, 2))],
        input_output_aliases={} if out is None else {1: 0},
        compiler_params=pltpu.CompilerParams(vmem_limit_bytes=VMEM_LIMIT),
        name="write_halves",
    )(value, *([] if out is None else [out]))


def shift_by(value, axis, offset):
    return lax.ppermute(value, axis, [(i, i ^ offset) for i in range(lax.axis_size(axis))])


def on_device(ingest, row_order, matrix_seeds):
    row_size, col_size = lax.axis_size("row"), lax.axis_size("col")
    _, depth = ingest.shape
    half = N // col_size // 2
    chips = row_size // 2

    peer = shift_by(ingest, "row", 1)
    peer_order = shift_by(row_order, "row", 1)
    by_column, by_n, by_row = tables(
        matrix_seeds, depth, col_size, half, chips, row_order.shape[1]
    )

    hints = [None] * col_size
    for s, count in ((1, col_size - 1), (0, 1)):
        parts = first_hint(ingest, peer, by_column, by_n, s, count, half, 1024, 512)
        for i, part in enumerate(parts):
            hints[s + i] = shift_by(part, "col", s + i) if s + i else part
    hint = sort_rows(hints, row_order, peer_order)
    sources = [hint]
    for t in range(1, chips):
        sources.append(shift_by(hint, "row", 2 * t))

    matrix = second_matrix(by_row, 0, 1, N)
    total = None
    for t in range(chips - 1):
        total, matrix = second_hint(sources[t], matrix, 0, N, total, by_row, t + 1)
    cut = N // 2
    totals = [second_hint(sources[-1], matrix, i * cut, cut, total)[0] for i in range(2)]

    others = [shift_by(value, "row", 1) for value in totals]
    out = None
    for flip, values in enumerate((totals, others)):
        for i, value in enumerate(values):
            out = write_halves(value, flip, i * cut, N, out)
    return out


def solution(mesh):
    in_specs = (P(("row", "col"), None), P("row", None), P())
    out_specs = P(None, None, "col", None)
    return jax.shard_map(
        on_device, mesh=mesh, in_specs=in_specs, out_specs=out_specs, check_vma=False
    )
```

```python
import functools

import jax
import jax.numpy as jnp
import numpy as np
from jax import lax
from jax.experimental import pallas as pl
from jax.experimental.pallas import tpu as pltpu
from jax.sharding import PartitionSpec as P


N = 1024

PRIME = 46337
HALF_PRIME = PRIME // 2
WHOLE = (1 << 32) // PRIME
PART = (1 << 32) / PRIME - WHOLE
SCALE = np.float32(PRIME / 2.0**32)
FINE = np.float32(1.5 * 2.0**23)
INVERSE = np.float32(1 / PRIME)
OFFSET = 32896 - HALF_PRIME
COARSE = np.float32(1.5 * 2.0**31 - 1.5 * 2.0**23 - OFFSET)
FINE_OFFSET = np.float32(1.5 * 2.0**23 + OFFSET)
SUBLANES = 16
VMEM_LIMIT = 16 << 20
LANES = 128
NT = (((1,), (1,)), ((), ()))


def residue(value):
    value = value - (value.astype(jnp.float32) * INVERSE).astype(jnp.int32) * PRIME
    value = value + jnp.where(value < 0, PRIME, 0)
    return value - jnp.where(value >= PRIME, PRIME, 0)


def centred(value):
    return value - jnp.where(value > HALF_PRIME, PRIME, 0)


def fixed(value):
    value = centred(value)
    return value * WHOLE + jnp.round(value.astype(jnp.float32) * np.float32(PART)).astype(jnp.int32)


def bend(step):
    value = 2 * (29989 * step % PRIME) ** 2 % PRIME
    value = value - PRIME if value > HALF_PRIME else value
    return np.int32(round(value * 2**32 / PRIME))


def by_first(index, seed, step):
    rows = 8
    shape = (rows, index.shape[1])
    row = lax.broadcasted_iota(jnp.int32, shape, 0)
    kind, second = row % 4, row >= 4
    start = jnp.where(second, 7919, 0) + seed
    a = residue(residue(residue(jnp.broadcast_to(index, shape)) * 40503) + start)
    a = residue(a * a)
    factor = 2 * (29989 * step % PRIME) % PRIME
    product = residue(a * jnp.where(kind == 1, a, factor))
    product = residue(product + jnp.where(kind == 1, 12345 - HALF_PRIME + PRIME, 0))
    return jnp.where(kind == 0, centred(a), fixed(product))


def by_second(index, step):
    shift = 29989 * step % PRIME
    b = residue(residue(index) * 29989)
    slope = residue(b * (2 * shift % PRIME))
    return [
        fixed(residue(2 * b)),
        fixed(residue(b * b)),
        fixed(residue(slope + shift * shift % PRIME)),
    ]


def tables_kernel(half, block_rows, seeds_ref, column_ref, n_ref, row_ref):
    row, col = lax.axis_index("row"), lax.axis_index("col")
    index = lax.broadcasted_iota(jnp.int32, (1, column_ref.shape[1]), 1)
    column_ref[...] = by_first(index, seeds_ref[0], SUBLANES)
    pair_rows = 2 * block_rows
    for t in range(row_ref.shape[0]):
        index = (row // 2 ^ t) * pair_rows + lax.broadcasted_iota(jnp.int32, (1, pair_rows), 1)
        row_ref[t] = by_first(index, seeds_ref[1], SUBLANES)
    sub = lax.broadcasted_iota(jnp.int32, (SUBLANES, LANES), 0)
    for s in range(n_ref.shape[0]):
        index = ((col ^ s) * 2 + row % 2) * half + sub
        for i, value in enumerate(by_second(index, SUBLANES)):
            n_ref[s, i] = value


def tables(seeds, depth, parts, half, chips, block_rows):
    return pl.pallas_call(
        functools.partial(tables_kernel, half, block_rows),
        out_shape=[
            jax.ShapeDtypeStruct((8, depth), jnp.int32),
            jax.ShapeDtypeStruct((parts, 3, SUBLANES, LANES), jnp.int32),
            jax.ShapeDtypeStruct((chips, 8, 2 * block_rows), jnp.int32),
        ],
        in_specs=[pl.BlockSpec(memory_space=pltpu.SMEM)],
        out_specs=[pl.BlockSpec(memory_space=pltpu.VMEM)] * 3,
        compiler_params=pltpu.CompilerParams(vmem_limit_bytes=VMEM_LIMIT),
        name="tables",
    )(seeds)


def limb_pair(value):
    rounded = value.astype(jnp.float32) * SCALE + FINE
    kept = (rounded + COARSE) - COARSE
    return (rounded - kept).astype(jnp.bfloat16), (kept - FINE_OFFSET).astype(jnp.bfloat16)


def join(products):
    low_p, high_p, low_q, high_q = (whole_number(product) for product in products)
    return low_p + (((low_q + (high_q << 8)) << 8) + high_p << 8)


def make_limbs(first_ref, second, start, width, lane, count, store, mixes=(0, 1)):
    second = [jnp.concatenate([value] * (lane // LANES), axis=1) for value in second]
    for t in range(width // lane):
        at = pl.ds(pl.multiple_of(start + t * lane, lane), lane)
        for mix in mixes:
            a, square, slope = (first_ref[4 * mix + i : 4 * mix + i + 1, at] for i in range(3))
            value = a * second[0] + square + second[1]
            slope = slope + second[2]
            for k in range(count):
                low, high = limb_pair(value)
                store(2 * mix, k * SUBLANES, t * lane, low)
                store(2 * mix + 1, k * SUBLANES, t * lane, high)
                value = value + slope
                slope = slope + bend(SUBLANES)


def first_kernel(offset, width, lane, own_ref, peer_ref, first_ref, second_ref, *refs):
    outs, even, odd = refs[:-2], refs[-2], refs[-1]
    half = outs[0].shape[0]
    total = own_ref.shape[1] // width
    small = jnp.bfloat16(1 / 256)

    def make(step, limbs):
        for s in range(len(outs)):

            def store(i, row, column, value):
                top = ((i % 2 * len(outs) + s) * 2 + i // 2) * half + row
                limbs[top : top + SUBLANES, column : column + lane] = value

            second = [second_ref[offset + s, i] for i in range(3)]
            make_limbs(first_ref, second, step * width, width, lane, half // SUBLANES, store)

    def use(step, limbs):
        at = pl.ds(pl.multiple_of(step * width, width), width)
        records = jnp.concatenate([own_ref[:, at], peer_ref[:, at]], axis=0)
        middle = limbs.shape[0] // 2
        low = lax.dot_general(limbs[:middle], records, NT, preferred_element_type=jnp.float32)
        high = lax.dot_general(
            limbs[middle:], records * small, NT, preferred_element_type=jnp.float32
        )
        for s, out_ref in enumerate(outs):
            p, q = (slice((2 * s + i) * half, (2 * s + i + 1) * half) for i in range(2))
            out_ref[...] += join([low[p], high[p], low[q], high[q]])

    for out_ref in outs:
        out_ref[...] = jnp.zeros_like(out_ref)
    make(0, even)

    @pl.loop(0, total // 2 - 1)
    def _(i):
        use(2 * i, even)
        make(2 * i + 1, odd)
        use(2 * i + 1, odd)
        make(2 * i + 2, even)

    use(total - 2, even)
    make(total - 1, odd)
    use(total - 1, odd)


def first_hint(own, peer, by_column, by_n, s, count, half, width, lane):
    rows, depth = own.shape
    width = min(width, depth)
    lane = min(lane, width)
    whole = pl.BlockSpec(memory_space=pltpu.VMEM)
    return pl.pallas_call(
        functools.partial(first_kernel, s, width, lane),
        out_shape=[jax.ShapeDtypeStruct((half, 2 * rows), jnp.int32)] * count,
        in_specs=[whole] * 4,
        out_specs=[whole] * count,
        scratch_shapes=[pltpu.VMEM((4 * count * half, width), jnp.bfloat16)] * 2,
        compiler_params=pltpu.CompilerParams(vmem_limit_bytes=VMEM_LIMIT),
        cost_estimate=pl.CostEstimate(
            flops=64 * count * half * depth * rows,
            bytes_accessed=4 * depth * rows,
            transcendentals=0,
        ),
        name="first_hint",
    )(own, peer, by_column, by_n)


def byte_digits(hint, place):
    byte = (lax.shift_right_logical(hint, jnp.int32(8 * place)) & 255) - 128
    return byte.astype(jnp.float32).astype(jnp.bfloat16)


def whole_number(value):
    return jnp.round(value).astype(jnp.int32)


def sort_kernel(pieces, *refs):
    hints, (own_ref, peer_ref, out_ref, digits, select) = refs[:pieces], refs[pieces:]
    core, col = lax.axis_index("row") % 2, lax.axis_index("col")
    half, rows = hints[0].shape
    block_rows = own_ref.shape[1]
    slice_rows = rows // 2
    for s, hint_ref in enumerate(hints):
        hint = hint_ref[...]
        for place in range(4):
            at = (slice(place * half, (place + 1) * half), slice(s * rows, (s + 1) * rows))
            digits[at] = byte_digits(hint, place)
    orders = [own_ref[...], peer_ref[...] + block_rows]
    swapped = core == 1
    target = jnp.concatenate(
        [
            jnp.where(swapped, orders[1], orders[0]),
            jnp.where(swapped, orders[0], orders[1]),
        ],
        axis=1,
    )
    for s in range(pieces):
        for e in range(2):
            start = e * block_rows + (col ^ s) * slice_rows
            row = start + lax.broadcasted_iota(jnp.int32, (slice_rows, 2 * block_rows), 0)
            top = s * rows + e * slice_rows
            select[top : top + slice_rows, :] = jnp.where(row == target, 1.0, 0.0).astype(
                jnp.bfloat16
            )
    hint = None
    for place in range(4):
        moved = jnp.dot(
            digits[place * half : (place + 1) * half],
            select[...],
            preferred_element_type=jnp.float32,
        )
        term = (whole_number(moved) + 128) << (8 * place)
        hint = term if hint is None else hint + term
    out_ref[...] = hint


def sort_rows(hints, own_order, peer_order):
    half, _ = hints[0].shape
    total = 2 * own_order.shape[1]
    whole = pl.BlockSpec(memory_space=pltpu.VMEM)
    return pl.pallas_call(
        functools.partial(sort_kernel, len(hints)),
        out_shape=jax.ShapeDtypeStruct((half, total), jnp.int32),
        in_specs=[whole] * (len(hints) + 2),
        out_specs=whole,
        scratch_shapes=[
            pltpu.VMEM((4 * half, total), jnp.bfloat16),
            pltpu.VMEM((total, total), jnp.bfloat16),
        ],
        compiler_params=pltpu.CompilerParams(vmem_limit_bytes=VMEM_LIMIT),
        name="sort_rows",
    )(*hints, own_order, peer_order)


def matrix_kernel(block, first_ref, *refs):
    out_ref = refs[-1]
    count, _, depth = first_ref.shape
    columns = out_ref.shape[1]
    lane = min(512, depth)
    sub = lax.broadcasted_iota(jnp.int32, (SUBLANES, LANES), 0)

    @pl.loop(0, columns // block)
    def _(i):
        start = pl.multiple_of(i * block, block)
        second = by_second(start + sub, SUBLANES)
        for t in range(count):

            def store(i, row, column, value):
                at = slice(t * depth + column, t * depth + column + lane)
                out_ref[i, pl.ds(start + row, SUBLANES), at] = value

            make_limbs(first_ref.at[t], second, 0, depth, lane, block // SUBLANES, store)


def second_matrix(by_row, group, count, columns, after=()):
    _, quantities, depth = by_row.shape
    block = min(128, columns)
    whole = pl.BlockSpec(memory_space=pltpu.VMEM)
    return pl.pallas_call(
        functools.partial(matrix_kernel, block),
        grid=(1,),
        out_shape=jax.ShapeDtypeStruct((4, columns, count * depth), jnp.bfloat16),
        in_specs=[pl.BlockSpec((count, quantities, depth), lambda i: (group, 0, 0))]
        + [pl.BlockSpec(memory_space=pl.ANY)] * len(after),
        out_specs=whole,
        compiler_params=pltpu.CompilerParams(vmem_limit_bytes=VMEM_LIMIT),
        cost_estimate=pl.CostEstimate(
            flops=2000 * count * depth * columns,
            bytes_accessed=8 * count * depth * columns,
            transcendentals=0,
        ),
        name="second_matrix",
    )(by_row, *after)


def spread(hint_refs, digits, small_digits):
    half = sum(ref.shape[0] for ref in hint_refs)
    for i, ref in enumerate(hint_refs):
        hint = ref[...]
        rows = ref.shape[0]
        for place in range(4):
            at = slice(place * half + i * rows, place * half + (i + 1) * rows)
            byte = byte_digits(hint, place)
            digits[at] = byte
            small_digits[at] = byte * jnp.bfloat16(1 / 256)


def product(digits, small_digits, matrix_ref, at):
    return join(
        [
            lax.dot_general(
                [digits, small_digits][limb % 2][...],
                matrix_ref[limb, at],
                NT,
                preferred_element_type=jnp.float32,
            )
            for limb in range(4)
        ]
    )


def second_kernel(block, count, has_total, *refs):
    hint_refs, (matrix_ref, next_ref) = refs[:count], refs[count : count + 2]
    total_ref = refs[count + 2] if has_total else None
    out_ref, next_matrix_ref, digits, small_digits = refs[-4:]
    _, half, columns = out_ref.shape
    depth = matrix_ref.shape[2]
    spread(hint_refs, digits, small_digits)
    sub = lax.broadcasted_iota(jnp.int32, (SUBLANES, LANES), 0)
    lane = min(512, depth)

    for start in range(0, columns, block):
        at = slice(start, start + block)

        def store(i, row, column, value, start=start):
            top = start + row
            next_matrix_ref[i, top : top + SUBLANES, column : column + lane] = value

        limbs = []
        second = by_second(start + sub, SUBLANES)
        for limb in range(4):
            limbs.append(
                lax.dot_general(
                    [digits, small_digits][limb % 2][...],
                    matrix_ref[limb, at],
                    NT,
                    preferred_element_type=jnp.float32,
                )
            )
            if limb % 2:
                make_limbs(next_ref, second, 0, depth, lane, block // SUBLANES, store, (limb // 2,))
        total = join(limbs)
        for place in range(4):
            term = total[place * half : (place + 1) * half]
            out_ref[place, :, at] = total_ref[place, :, at] + term if has_total else term


def product_cost(rows, depth, columns):
    return pl.CostEstimate(
        flops=8 * rows * depth * columns,
        bytes_accessed=8 * depth * columns + 8 * rows * columns,
        transcendentals=0,
    )


def second_hint(hints, matrix, by_row, t, total=None):
    half = sum(hint.shape[0] for hint in hints)
    _, columns, depth = matrix.shape
    has_total = total is not None
    whole = pl.BlockSpec(memory_space=pltpu.VMEM)
    row_spec = pl.BlockSpec((None,) + by_row.shape[1:], lambda i: (t, 0, 0))
    return pl.pallas_call(
        functools.partial(second_kernel, min(256, columns), len(hints), has_total),
        grid=(1,),
        out_shape=[
            jax.ShapeDtypeStruct((4, half, columns), jnp.int32),
            jax.ShapeDtypeStruct(matrix.shape, matrix.dtype),
        ],
        in_specs=[whole] * (len(hints) + 1) + [row_spec] + [whole] * has_total,
        out_specs=[whole] * 2,
        scratch_shapes=[pltpu.VMEM((4 * half, depth), jnp.bfloat16)] * 2,
        compiler_params=pltpu.CompilerParams(vmem_limit_bytes=VMEM_LIMIT),
        cost_estimate=product_cost(4 * half, depth, columns),
        name="second_hint",
    )(*hints, matrix, by_row, *([total] if has_total else []))


def own_rows(half, flip):
    core = lax.axis_index("row") % 2
    return pl.ds(pl.multiple_of((1 - core if flip else core) * half, half), half)


def put_halves(value, out_ref, place, rows, columns, low, high, sems):
    scale = np.float32(1 / 65536)
    low[...] = (value & 65535).astype(jnp.float32) * scale
    high[...] = lax.shift_right_logical(value, jnp.int32(16)).astype(jnp.float32) * scale
    copies = []
    for k, source in enumerate((low, high)):
        target = out_ref.at[place, k, rows, columns]
        copies.append(pltpu.make_async_copy(source, target, sems.at[k]))
        copies[-1].start()
    return copies


def last_kernel(block, first, count, *refs):
    hint_refs, (matrix_ref, total_ref, sum_ref, digits, small_digits) = refs[:count], refs[count:]
    _, half, columns = sum_ref.shape
    spread(hint_refs, digits, small_digits)
    for i in range(columns // block):
        inner = slice(i * block, (i + 1) * block)
        at = slice(first + i * block, first + (i + 1) * block)
        total = product(digits, small_digits, matrix_ref, at)
        for place in range(4):
            term = total[place * half : (place + 1) * half]
            sum_ref[place, :, inner] = total_ref[place, :, at] + term


def last_hint(hints, matrix, total, first, count):
    half = sum(hint.shape[0] for hint in hints)
    depth = matrix.shape[2]
    whole = pl.BlockSpec(memory_space=pltpu.VMEM)
    return pl.pallas_call(
        functools.partial(last_kernel, min(256, count), first, len(hints)),
        in_specs=[whole] * (len(hints) + 2),
        out_specs=whole,
        out_shape=jax.ShapeDtypeStruct((4, half, count), jnp.int32),
        scratch_shapes=[pltpu.VMEM((4 * half, depth), jnp.bfloat16)] * 2,
        compiler_params=pltpu.CompilerParams(vmem_limit_bytes=VMEM_LIMIT),
        cost_estimate=product_cost(4 * half, depth, count),
        name="last_hint",
    )(*hints, matrix, total)


def halves_scratch(shape):
    return [pltpu.VMEM(shape, jnp.float32)] * 2 + [pltpu.SemaphoreType.DMA((shape[0], 2))]


def write_part(value_ref, out_ref, flip, first, low, high, sems):
    digits, half, columns = value_ref.shape
    rows, at = own_rows(half, flip), pl.ds(first, columns)
    copies = []
    for i in range(digits):
        copies += put_halves(
            value_ref[i], out_ref, i, rows, at, low.at[i], high.at[i], sems.at[i]
        )
    return copies


def write_kernel(parts, *refs):
    scratch = refs[len(refs) - 3 * len(parts) :]
    out_ref = refs[len(refs) - 3 * len(parts) - 1]
    copies = []
    for i, (flip, first) in enumerate(parts):
        copies += write_part(refs[i], out_ref, flip, first, *scratch[3 * i : 3 * i + 3])
    for copy in copies:
        copy.wait()


def write_parts(values, parts, columns, out=None):
    digits, half, _ = values[0].shape
    anywhere = pl.BlockSpec(memory_space=pl.ANY)
    has_out = out is not None
    return pl.pallas_call(
        functools.partial(write_kernel, parts),
        in_specs=[pl.BlockSpec(memory_space=pltpu.VMEM)] * len(values) + [anywhere] * has_out,
        out_specs=anywhere,
        out_shape=jax.ShapeDtypeStruct((digits, 2, 2 * half, columns), jnp.float32),
        scratch_shapes=[scratch for value in values for scratch in halves_scratch(value.shape)],
        input_output_aliases={len(values): 0} if has_out else {},
        compiler_params=pltpu.CompilerParams(vmem_limit_bytes=VMEM_LIMIT),
        name="write_parts",
    )(*values, *([out] if has_out else []))


def shift_by(value, axis, offset):
    return lax.ppermute(value, axis, [(i, i ^ offset) for i in range(lax.axis_size(axis))])


def on_device(ingest, row_order, matrix_seeds):
    row_size, col_size = lax.axis_size("row"), lax.axis_size("col")
    _, depth = ingest.shape
    half = N // col_size // 2
    chips = row_size // 2

    peer = shift_by(ingest, "row", 1)
    peer_order = shift_by(row_order, "row", 1)
    by_column, by_n, by_row = tables(
        matrix_seeds, depth, col_size, half, chips, row_order.shape[1]
    )

    hints = [None] * col_size
    for s, count in ((1, col_size - 1), (0, 1)):
        parts = first_hint(ingest, peer, by_column, by_n, s, count, half, 1024, 512)
        for i, part in enumerate(parts):
            hints[s + i] = shift_by(part, "col", s + i) if s + i else part
    hint = sort_rows(hints, row_order, peer_order)
    sources = [[hint]]
    for t in range(1, chips):
        low = t & -t
        if low == t:
            sources.append([shift_by(hint, "row", 2 * t)])
            continue
        halves = []
        for i, (via, rest) in enumerate(((low, t ^ low), (t ^ low, low))):
            piece = jnp.concatenate(sources[rest]) if len(sources[rest]) > 1 else sources[rest][0]
            piece = piece[i * (half // 2) : (i + 1) * (half // 2)]
            halves.append(shift_by(piece, "row", 2 * via))
        sources.append(halves)

    matrix = second_matrix(by_row, 0, 1, N)
    total = None
    for t in range(chips - 1):
        total, matrix = second_hint(sources[t], matrix, by_row, t + 1, total)
    cut = N // 2
    sums = [last_hint(sources[-1], matrix, total, i * cut, cut) for i in range(2)]
    others = [shift_by(value, "row", 1) for value in sums]
    out = write_parts(sums, [(False, 0), (False, cut)], N)
    return write_parts(others, [(True, 0), (True, cut)], N, out)


def solution(mesh):
    in_specs = (P(("row", "col"), None), P("row", None), P())
    out_specs = P(None, None, "col", None)
    return jax.shard_map(
        on_device, mesh=mesh, in_specs=in_specs, out_specs=out_specs, check_vma=False
    )
```

```python
import functools

import jax
import jax.numpy as jnp
import numpy as np
from jax import lax
from jax.experimental import pallas as pl
from jax.experimental.pallas import tpu as pltpu
from jax.sharding import PartitionSpec as P


N = 1024

PRIME = 46337
HALF_PRIME = PRIME // 2
WHOLE = (1 << 32) // PRIME
PART = (1 << 32) / PRIME - WHOLE
SCALE = np.float32(PRIME / 2.0**32)
FINE = np.float32(1.5 * 2.0**23)
INVERSE = np.float32(1 / PRIME)
OFFSET = 32896 - HALF_PRIME
COARSE = np.float32(1.5 * 2.0**31 - 1.5 * 2.0**23 - OFFSET)
FINE_OFFSET = np.float32(1.5 * 2.0**23 + OFFSET)
SUBLANES = 16
VMEM_LIMIT = 16 << 20
LANES = 128
NT = (((1,), (1,)), ((), ()))


def residue(value):
    value = value - (value.astype(jnp.float32) * INVERSE).astype(jnp.int32) * PRIME
    value = value + jnp.where(value < 0, PRIME, 0)
    return value - jnp.where(value >= PRIME, PRIME, 0)


def centred(value):
    return value - jnp.where(value > HALF_PRIME, PRIME, 0)


def fixed(value):
    value = centred(value)
    return value * WHOLE + jnp.round(value.astype(jnp.float32) * np.float32(PART)).astype(jnp.int32)


def bend(step):
    value = 2 * (29989 * step % PRIME) ** 2 % PRIME
    value = value - PRIME if value > HALF_PRIME else value
    return np.int32(round(value * 2**32 / PRIME))


def by_first(index, seed, step):
    rows = 8
    shape = (rows, index.shape[1])
    row = lax.broadcasted_iota(jnp.int32, shape, 0)
    kind, second = row % 4, row >= 4
    start = jnp.where(second, 7919, 0) + seed
    a = residue(residue(residue(jnp.broadcast_to(index, shape)) * 40503) + start)
    a = residue(a * a)
    factor = 2 * (29989 * step % PRIME) % PRIME
    product = residue(a * jnp.where(kind == 1, a, factor))
    product = residue(product + jnp.where(kind == 1, 12345 - HALF_PRIME + PRIME, 0))
    return jnp.where(kind == 0, centred(a), fixed(product))


def by_second(index, step):
    shift = 29989 * step % PRIME
    b = residue(residue(index) * 29989)
    slope = residue(b * (2 * shift % PRIME))
    return [
        fixed(residue(2 * b)),
        fixed(residue(b * b)),
        fixed(residue(slope + shift * shift % PRIME)),
    ]


def tables_kernel(half, block_rows, seeds_ref, column_ref, n_ref, row_ref):
    row, col = lax.axis_index("row"), lax.axis_index("col")
    index = lax.broadcasted_iota(jnp.int32, (1, column_ref.shape[1]), 1)
    column_ref[...] = by_first(index, seeds_ref[0], SUBLANES)
    pair_rows = 2 * block_rows
    for t in range(row_ref.shape[0]):
        index = (row // 2 ^ t) * pair_rows + lax.broadcasted_iota(jnp.int32, (1, pair_rows), 1)
        row_ref[t] = by_first(index, seeds_ref[1], SUBLANES)
    sub = lax.broadcasted_iota(jnp.int32, (SUBLANES, LANES), 0)
    for s in range(n_ref.shape[0]):
        index = ((col ^ s) * 2 + row % 2) * half + sub
        for i, value in enumerate(by_second(index, SUBLANES)):
            n_ref[s, i] = value


def tables(seeds, depth, parts, half, chips, block_rows):
    return pl.pallas_call(
        functools.partial(tables_kernel, half, block_rows),
        out_shape=[
            jax.ShapeDtypeStruct((8, depth), jnp.int32),
            jax.ShapeDtypeStruct((parts, 3, SUBLANES, LANES), jnp.int32),
            jax.ShapeDtypeStruct((chips, 8, 2 * block_rows), jnp.int32),
        ],
        in_specs=[pl.BlockSpec(memory_space=pltpu.SMEM)],
        out_specs=[pl.BlockSpec(memory_space=pltpu.VMEM)] * 3,
        compiler_params=pltpu.CompilerParams(vmem_limit_bytes=VMEM_LIMIT),
        name="tables",
    )(seeds)


def limb_pair(value):
    rounded = value.astype(jnp.float32) * SCALE + FINE
    kept = (rounded + COARSE) - COARSE
    return (rounded - kept).astype(jnp.bfloat16), (kept - FINE_OFFSET).astype(jnp.bfloat16)


def join(products):
    low_p, high_p, low_q, high_q = (whole_number(product) for product in products)
    return low_p + (((low_q + (high_q << 8)) << 8) + high_p << 8)


def make_limbs(first_ref, second, start, width, lane, count, store, mixes=(0, 1)):
    second = [jnp.concatenate([value] * (lane // LANES), axis=1) for value in second]
    for t in range(width // lane):
        at = pl.ds(pl.multiple_of(start + t * lane, lane), lane)
        for mix in mixes:
            a, square, slope = (first_ref[4 * mix + i : 4 * mix + i + 1, at] for i in range(3))
            value = a * second[0] + square + second[1]
            slope = slope + second[2]
            for k in range(count):
                low, high = limb_pair(value)
                store(2 * mix, k * SUBLANES, t * lane, low)
                store(2 * mix + 1, k * SUBLANES, t * lane, high)
                value = value + slope
                slope = slope + bend(SUBLANES)


def first_kernel(offset, width, lane, own_ref, peer_ref, first_ref, second_ref, *refs):
    outs, even, odd = refs[:-2], refs[-2], refs[-1]
    half = outs[0].shape[0]
    total = own_ref.shape[1] // width
    small = jnp.bfloat16(1 / 256)

    def make(step, limbs):
        for s in range(len(outs)):

            def store(i, row, column, value):
                top = ((i % 2 * len(outs) + s) * 2 + i // 2) * half + row
                limbs[top : top + SUBLANES, column : column + lane] = value

            second = [second_ref[offset + s, i] for i in range(3)]
            make_limbs(first_ref, second, step * width, width, lane, half // SUBLANES, store)

    def use(step, limbs):
        at = pl.ds(pl.multiple_of(step * width, width), width)
        records = jnp.concatenate([own_ref[:, at], peer_ref[:, at]], axis=0)
        middle = limbs.shape[0] // 2
        low = lax.dot_general(limbs[:middle], records, NT, preferred_element_type=jnp.float32)
        high = lax.dot_general(
            limbs[middle:], records * small, NT, preferred_element_type=jnp.float32
        )
        for s, out_ref in enumerate(outs):
            p, q = (slice((2 * s + i) * half, (2 * s + i + 1) * half) for i in range(2))
            out_ref[...] += join([low[p], high[p], low[q], high[q]])

    for out_ref in outs:
        out_ref[...] = jnp.zeros_like(out_ref)
    make(0, even)

    @pl.loop(0, total // 2 - 1)
    def _(i):
        use(2 * i, even)
        make(2 * i + 1, odd)
        use(2 * i + 1, odd)
        make(2 * i + 2, even)

    use(total - 2, even)
    make(total - 1, odd)
    use(total - 1, odd)


def first_hint(own, peer, by_column, by_n, s, count, half, width, lane):
    rows, depth = own.shape
    width = min(width, depth)
    lane = min(lane, width)
    whole = pl.BlockSpec(memory_space=pltpu.VMEM)
    return pl.pallas_call(
        functools.partial(first_kernel, s, width, lane),
        out_shape=[jax.ShapeDtypeStruct((half, 2 * rows), jnp.int32)] * count,
        in_specs=[whole] * 4,
        out_specs=[whole] * count,
        scratch_shapes=[pltpu.VMEM((4 * count * half, width), jnp.bfloat16)] * 2,
        compiler_params=pltpu.CompilerParams(vmem_limit_bytes=VMEM_LIMIT),
        cost_estimate=pl.CostEstimate(
            flops=64 * count * half * depth * rows,
            bytes_accessed=4 * depth * rows,
            transcendentals=0,
        ),
        name="first_hint",
    )(own, peer, by_column, by_n)


def byte_digits(hint, place):
    byte = (lax.shift_right_logical(hint, jnp.int32(8 * place)) & 255) - 128
    return byte.astype(jnp.float32).astype(jnp.bfloat16)


def whole_number(value):
    return jnp.round(value).astype(jnp.int32)


def sort_kernel(pieces, *refs):
    hints, (own_ref, peer_ref, out_ref, digits, select) = refs[:pieces], refs[pieces:]
    core, col = lax.axis_index("row") % 2, lax.axis_index("col")
    half, rows = hints[0].shape
    block_rows = own_ref.shape[1]
    slice_rows = rows // 2
    for s, hint_ref in enumerate(hints):
        hint = hint_ref[...]
        for place in range(4):
            at = (slice(place * half, (place + 1) * half), slice(s * rows, (s + 1) * rows))
            digits[at] = byte_digits(hint, place)
    orders = [own_ref[...], peer_ref[...] + block_rows]
    swapped = core == 1
    target = jnp.concatenate(
        [
            jnp.where(swapped, orders[1], orders[0]),
            jnp.where(swapped, orders[0], orders[1]),
        ],
        axis=1,
    )
    for s in range(pieces):
        for e in range(2):
            start = e * block_rows + (col ^ s) * slice_rows
            row = start + lax.broadcasted_iota(jnp.int32, (slice_rows, 2 * block_rows), 0)
            top = s * rows + e * slice_rows
            select[top : top + slice_rows, :] = jnp.where(row == target, 1.0, 0.0).astype(
                jnp.bfloat16
            )
    hint = None
    for place in range(4):
        moved = jnp.dot(
            digits[place * half : (place + 1) * half],
            select[...],
            preferred_element_type=jnp.float32,
        )
        term = (whole_number(moved) + 128) << (8 * place)
        hint = term if hint is None else hint + term
    out_ref[...] = hint


def sort_rows(hints, own_order, peer_order):
    half, _ = hints[0].shape
    total = 2 * own_order.shape[1]
    whole = pl.BlockSpec(memory_space=pltpu.VMEM)
    return pl.pallas_call(
        functools.partial(sort_kernel, len(hints)),
        out_shape=jax.ShapeDtypeStruct((half, total), jnp.int32),
        in_specs=[whole] * (len(hints) + 2),
        out_specs=whole,
        scratch_shapes=[
            pltpu.VMEM((4 * half, total), jnp.bfloat16),
            pltpu.VMEM((total, total), jnp.bfloat16),
        ],
        compiler_params=pltpu.CompilerParams(vmem_limit_bytes=VMEM_LIMIT),
        name="sort_rows",
    )(*hints, own_order, peer_order)


def matrix_kernel(block, first_ref, *refs):
    out_ref = refs[-1]
    count, _, depth = first_ref.shape
    columns = out_ref.shape[1]
    lane = min(512, depth)
    sub = lax.broadcasted_iota(jnp.int32, (SUBLANES, LANES), 0)

    @pl.loop(0, columns // block)
    def _(i):
        start = pl.multiple_of(i * block, block)
        second = by_second(start + sub, SUBLANES)
        for t in range(count):

            def store(i, row, column, value):
                at = slice(t * depth + column, t * depth + column + lane)
                out_ref[i, pl.ds(start + row, SUBLANES), at] = value

            make_limbs(first_ref.at[t], second, 0, depth, lane, block // SUBLANES, store)


def second_matrix(by_row, group, count, columns, after=()):
    _, quantities, depth = by_row.shape
    block = min(128, columns)
    whole = pl.BlockSpec(memory_space=pltpu.VMEM)
    return pl.pallas_call(
        functools.partial(matrix_kernel, block),
        grid=(1,),
        out_shape=jax.ShapeDtypeStruct((4, columns, count * depth), jnp.bfloat16),
        in_specs=[pl.BlockSpec((count, quantities, depth), lambda i: (group, 0, 0))]
        + [pl.BlockSpec(memory_space=pl.ANY)] * len(after),
        out_specs=whole,
        compiler_params=pltpu.CompilerParams(vmem_limit_bytes=VMEM_LIMIT),
        cost_estimate=pl.CostEstimate(
            flops=2000 * count * depth * columns,
            bytes_accessed=8 * count * depth * columns,
            transcendentals=0,
        ),
        name="second_matrix",
    )(by_row, *after)


def spread(hint_refs, digits, small_digits):
    half = sum(ref.shape[0] for ref in hint_refs)
    for i, ref in enumerate(hint_refs):
        hint = ref[...]
        rows = ref.shape[0]
        for place in range(4):
            at = slice(place * half + i * rows, place * half + (i + 1) * rows)
            byte = byte_digits(hint, place)
            digits[at] = byte
            small_digits[at] = byte * jnp.bfloat16(1 / 256)


def product(digits, small_digits, matrix_ref, at):
    return join(
        [
            lax.dot_general(
                [digits, small_digits][limb % 2][...],
                matrix_ref[limb, at],
                NT,
                preferred_element_type=jnp.float32,
            )
            for limb in range(4)
        ]
    )


def second_kernel(block, count, has_total, *refs):
    hint_refs, (matrix_ref, next_ref) = refs[:count], refs[count : count + 2]
    total_ref = refs[count + 2] if has_total else None
    out_ref, next_matrix_ref, digits, small_digits = refs[-4:]
    _, half, columns = out_ref.shape
    depth = matrix_ref.shape[2]
    spread(hint_refs, digits, small_digits)
    sub = lax.broadcasted_iota(jnp.int32, (SUBLANES, LANES), 0)
    lane = min(512, depth)

    for start in range(0, columns, block):
        at = slice(start, start + block)

        def store(i, row, column, value, start=start):
            top = start + row
            next_matrix_ref[i, top : top + SUBLANES, column : column + lane] = value

        limbs = []
        second = by_second(start + sub, SUBLANES)
        for limb in range(4):
            limbs.append(
                lax.dot_general(
                    [digits, small_digits][limb % 2][...],
                    matrix_ref[limb, at],
                    NT,
                    preferred_element_type=jnp.float32,
                )
            )
            if limb % 2:
                make_limbs(next_ref, second, 0, depth, lane, block // SUBLANES, store, (limb // 2,))
        total = join(limbs)
        for place in range(4):
            term = total[place * half : (place + 1) * half]
            out_ref[place, :, at] = total_ref[place, :, at] + term if has_total else term


def product_cost(rows, depth, columns):
    return pl.CostEstimate(
        flops=8 * rows * depth * columns,
        bytes_accessed=8 * depth * columns + 8 * rows * columns,
        transcendentals=0,
    )


def second_hint(hints, matrix, by_row, t, total=None):
    half = sum(hint.shape[0] for hint in hints)
    _, columns, depth = matrix.shape
    has_total = total is not None
    whole = pl.BlockSpec(memory_space=pltpu.VMEM)
    row_spec = pl.BlockSpec((None,) + by_row.shape[1:], lambda i: (t, 0, 0))
    return pl.pallas_call(
        functools.partial(second_kernel, min(256, columns), len(hints), has_total),
        grid=(1,),
        out_shape=[
            jax.ShapeDtypeStruct((4, half, columns), jnp.int32),
            jax.ShapeDtypeStruct(matrix.shape, matrix.dtype),
        ],
        in_specs=[whole] * (len(hints) + 1) + [row_spec] + [whole] * has_total,
        out_specs=[whole] * 2,
        scratch_shapes=[pltpu.VMEM((4 * half, depth), jnp.bfloat16)] * 2,
        compiler_params=pltpu.CompilerParams(vmem_limit_bytes=VMEM_LIMIT),
        cost_estimate=product_cost(4 * half, depth, columns),
        name="second_hint",
    )(*hints, matrix, by_row, *([total] if has_total else []))


def own_rows(half, flip):
    core = lax.axis_index("row") % 2
    return pl.ds(pl.multiple_of((1 - core if flip else core) * half, half), half)


def put_halves(value, out_ref, place, rows, columns, low, high, sems):
    scale = np.float32(1 / 65536)
    low[...] = (value & 65535).astype(jnp.float32) * scale
    high[...] = lax.shift_right_logical(value, jnp.int32(16)).astype(jnp.float32) * scale
    copies = []
    for k, source in enumerate((low, high)):
        target = out_ref.at[place, k, rows, columns]
        copies.append(pltpu.make_async_copy(source, target, sems.at[k]))
        copies[-1].start()
    return copies


def last_kernel(block, first, count, *refs):
    hint_refs, refs = refs[:count], refs[count:]
    if count:
        matrix_ref, total_ref, sum_ref, digits, small_digits = refs
        spread(hint_refs, digits, small_digits)
    else:
        digits, small_digits, matrix_ref, total_ref, sum_ref = refs
    _, half, columns = sum_ref.shape
    for i in range(columns // block):
        inner = slice(i * block, (i + 1) * block)
        at = slice(first + i * block, first + (i + 1) * block)
        total = product(digits, small_digits, matrix_ref, at)
        for place in range(4):
            term = total[place * half : (place + 1) * half]
            sum_ref[place, :, inner] = total_ref[place, :, at] + term


def last_hint(hints, matrix, total, first, count, digits=()):
    half = total.shape[1]
    depth = matrix.shape[2]
    whole = pl.BlockSpec(memory_space=pltpu.VMEM)
    sources = list(digits) or list(hints)
    extra = 0 if digits else 2
    return pl.pallas_call(
        functools.partial(last_kernel, min(256, count), first, 0 if digits else len(hints)),
        in_specs=[whole] * (len(sources) + 2),
        out_specs=[whole] * (1 + extra),
        out_shape=[jax.ShapeDtypeStruct((4, half, count), jnp.int32)]
        + [jax.ShapeDtypeStruct((4 * half, depth), jnp.bfloat16)] * extra,
        compiler_params=pltpu.CompilerParams(vmem_limit_bytes=VMEM_LIMIT),
        cost_estimate=product_cost(4 * half, depth, count),
        name="last_hint",
    )(*sources, matrix, total)


def halves_scratch(shape):
    return [pltpu.VMEM(shape, jnp.float32)] * 2 + [pltpu.SemaphoreType.DMA((shape[0], 2))]


def write_part(value_ref, out_ref, flip, first, low, high, sems):
    digits, half, columns = value_ref.shape
    rows, at = own_rows(half, flip), pl.ds(first, columns)
    copies = []
    for i in range(digits):
        copies += put_halves(
            value_ref[i], out_ref, i, rows, at, low.at[i], high.at[i], sems.at[i]
        )
    return copies


def write_kernel(parts, *refs):
    scratch = refs[len(refs) - 3 * len(parts) :]
    out_ref = refs[len(refs) - 3 * len(parts) - 1]
    copies = []
    for i, (flip, first) in enumerate(parts):
        copies += write_part(refs[i], out_ref, flip, first, *scratch[3 * i : 3 * i + 3])
    for copy in copies:
        copy.wait()


def write_parts(values, parts, columns, out=None):
    digits, half, _ = values[0].shape
    anywhere = pl.BlockSpec(memory_space=pl.ANY)
    has_out = out is not None
    return pl.pallas_call(
        functools.partial(write_kernel, parts),
        in_specs=[pl.BlockSpec(memory_space=pltpu.VMEM)] * len(values) + [anywhere] * has_out,
        out_specs=anywhere,
        out_shape=jax.ShapeDtypeStruct((digits, 2, 2 * half, columns), jnp.float32),
        scratch_shapes=[scratch for value in values for scratch in halves_scratch(value.shape)],
        input_output_aliases={len(values): 0} if has_out else {},
        compiler_params=pltpu.CompilerParams(vmem_limit_bytes=VMEM_LIMIT),
        name="write_parts",
    )(*values, *([out] if has_out else []))


def shift_by(value, axis, offset):
    return lax.ppermute(value, axis, [(i, i ^ offset) for i in range(lax.axis_size(axis))])


def on_device(ingest, row_order, matrix_seeds):
    row_size, col_size = lax.axis_size("row"), lax.axis_size("col")
    _, depth = ingest.shape
    half = N // col_size // 2
    chips = row_size // 2

    peer = shift_by(ingest, "row", 1)
    peer_order = shift_by(row_order, "row", 1)
    by_column, by_n, by_row = tables(
        matrix_seeds, depth, col_size, half, chips, row_order.shape[1]
    )

    hints = [None] * col_size
    for s, count in ((1, col_size - 1), (0, 1)):
        parts = first_hint(ingest, peer, by_column, by_n, s, count, half, 1024, 512)
        for i, part in enumerate(parts):
            hints[s + i] = shift_by(part, "col", s + i) if s + i else part
    hint = sort_rows(hints, row_order, peer_order)
    sources = [[hint]]
    for t in range(1, chips):
        low = t & -t
        if low == t:
            sources.append([shift_by(hint, "row", 2 * t)])
            continue
        halves = []
        for i, (via, rest) in enumerate(((low, t ^ low), (t ^ low, low))):
            piece = jnp.concatenate(sources[rest]) if len(sources[rest]) > 1 else sources[rest][0]
            piece = piece[i * (half // 2) : (i + 1) * (half // 2)]
            halves.append(shift_by(piece, "row", 2 * via))
        sources.append(halves)

    matrix = second_matrix(by_row, 0, 1, N)
    total = None
    for t in range(chips - 1):
        total, matrix = second_hint(sources[t], matrix, by_row, t + 1, total)
    cut = N // 2
    early, *digits = last_hint(sources[-1], matrix, total, 0, cut)
    (late,) = last_hint(sources[-1], matrix, total, cut, cut, digits)
    sums = [early, late]
    others = [shift_by(value, "row", 1) for value in sums]
    out = write_parts(sums, [(False, 0), (False, cut)], N)
    return write_parts(others, [(True, 0), (True, cut)], N, out)


def solution(mesh):
    in_specs = (P(("row", "col"), None), P("row", None), P())
    out_specs = P(None, None, "col", None)
    return jax.shard_map(
        on_device, mesh=mesh, in_specs=in_specs, out_specs=out_specs, check_vma=False
    )
```
